256 devices in a mesh: row: 8 (over z_lo, y), col: 16 (over x, z_hi), rep: 2 (over core).
Axes of the slice: x: 4, y: 4, z: 8 (z_hi: 4, z_lo: 2; z = z_hi * 2 + z_lo), core: 2. Of those that a mesh axis runs over, the one named last changes fastest.
Arguments:
- streams: bfloat16 [16384, 4, 2048], P(('row', 'col', 'rep')), may hold values from -6 to 6
- lengths: int32 [8], P('row'), may hold values from 1 to 4096, as said below
- cache: bfloat16 [8, 16, 4096, 256], P('row', 'col', 'rep'), may hold values from -1000 to 1000, as said below
- hc_static: float32 [2, 4, 6], replicated, may hold values from -2 to 3
- hc_dynamic: bfloat16 [2, 2048, 6], replicated, may hold values from -0.125 to 0.125
- w_qkv: bfloat16 [2048, 16, 384], P('row', 'col'), may hold values from -0.125 to 0.125
- w_out: bfloat16 [2048, 2048], P('row', 'col'), may hold values from -0.125 to 0.125
- w_gate_up: bfloat16 [2048, 2, 8192], P('row', None, 'col'), may hold values from -0.125 to 0.125
- w_down: bfloat16 [2048, 8192], P('row', 'col'), may hold values from -0.0625 to 0.0625
Outputs:
- new_streams: bfloat16 [16384, 4, 2048], P(('row', 'col', 'rep'))
- decode_cache: bfloat16 [8, 2, 16, 2048, 256], P('row', None, 'rep', 'col')
- decode_new: bfloat16 [8, 2, 16, 1024, 256], P('row', None, 'rep', 'col')
The draws below stay inside these ranges and needn't reach their ends.
Inputs may be any that keep to these rules, and one draw needn't show every extreme that they name: lengths[r] counts the valid cached positions of prompt r; in every draw one prompt's cache is full (4096 positions). cache positions at or after lengths[r] are not attended.
All inputs are finite; a program needn't handle non-finite values.
Results may differ from the reference program's by a relative error of at most 0.017.
Values may be sent and summed in bfloat16 or wider, within the bound.
A program may use at most 128 MiB of HBM per device.

```python
import math
import jax
import jax.numpy as jnp
from jax import lax

D = 2048
HEADS = 16
HD = 128
FF = 8192
STREAMS = 4
TOK_DEV = 64
CACHE_DEV = 2048
PROMPTS = 8
STRETCH = 2048
CACHE = 4096
TOKENS = 16384
N_COL = 16
N_REP = 2


def draw_lengths(key, part):
    key_one, key_two, key_three = jax.random.split(key, 3)
    levels = jax.random.randint(key_one, (PROMPTS,), 0, 4)
    longest = jnp.right_shift(jnp.full((PROMPTS,), CACHE, jnp.int32), levels.astype(jnp.int32))
    trimmed = longest - jax.random.randint(key_two, (PROMPTS,), 0, CACHE // 16)
    trimmed = jnp.maximum(trimmed, 1)
    chosen = jax.random.randint(key_three, (), 0, PROMPTS)
    return jnp.where(jnp.arange(PROMPTS, dtype=jnp.int32) == chosen, CACHE, trimmed).astype(jnp.int32)


def draw_cache(key, part):
    key_one = jax.random.fold_in(key, 0)
    base = jax.random.normal(key_one, (PROMPTS, HEADS, CACHE, 2 * HD), jnp.float32)
    return jnp.clip(base, -1000.0, 1000.0).astype(jnp.bfloat16)


def draw_hc_static(key, part):
    shape_all = (2, STREAMS, STREAMS + 2)
    layer_ids = lax.broadcasted_iota(jnp.int32, shape_all, 0)
    stream_ids = lax.broadcasted_iota(jnp.int32, shape_all, 1)
    column_ids = lax.broadcasted_iota(jnp.int32, shape_all, 2)
    width_part = jnp.where(stream_ids == layer_ids, 1.0, 0.0)
    mixing_part = jnp.where(column_ids - 1 == stream_ids, 1.0, 0.0)
    base = jnp.where(column_ids == 0, width_part, jnp.where(column_ids == STREAMS + 1, 1.0, mixing_part))
    noise = 0.3 * jax.random.normal(key, shape_all, jnp.float32)
    return jnp.clip(base + noise, -2.0, 3.0).astype(jnp.float32)


def shard_levels(own_key, extent, cuts, smallest, high):
    level, own = 1.0, jax.random.fold_in(own_key, 6)
    for dim, shards_of in cuts:
        draws = jnp.exp(jax.random.uniform(jax.random.fold_in(own, dim), (shards_of,), jnp.float32, smallest / len(cuts), high / len(cuts)))
        level = level * jnp.repeat(draws, extent[dim] // shards_of).reshape([-1 if axis == dim else 1 for axis in range(len(extent))])
    return level


def bell_draw(key, shape, scale, reach, cuts=(), held_as=jnp.bfloat16):
    factor_of = shard_levels(key, shape, cuts, -0.22, 0.18) if cuts else 1.0
    drawn = jax.random.normal(key, shape, jnp.float32) * scale * factor_of
    return jnp.minimum(jnp.maximum(drawn, -reach), reach).astype(held_as)


def setup_inputs(seed: int = 0) -> dict:
    key_of = jax.random.split(jax.random.key(seed), 10)
    return {
        "streams": bell_draw(key_of[0], (TOKENS, STREAMS, D), 1.0, 6.0, ((0, 256),)),
        "lengths": draw_lengths(jax.random.fold_in(key_of[9], 71), 0),
        "cache": draw_cache(jax.random.fold_in(key_of[9], 71), 0),
        "hc_static": draw_hc_static(jax.random.fold_in(key_of[9], 71), 0),
        "hc_dynamic": bell_draw(key_of[4], (2, D, STREAMS + 2), D ** -0.5, 0.125),
        "w_qkv": bell_draw(key_of[5], (D, HEADS, 3 * HD), D ** -0.5, 0.125, ((0, 8), (1, 16))),
        "w_out": bell_draw(key_of[6], (D, HEADS * HD), (HEADS * HD) ** -0.5, 0.125, ((0, 8), (1, 16))),
        "w_gate_up": bell_draw(key_of[7], (D, 2, FF), D ** -0.5, 0.125, ((0, 8), (2, 16))),
        "w_down": bell_draw(key_of[8], (D, FF), FF ** -0.5, 0.0625, ((0, 8), (1, 16))),
    }


EPS = 1e-05
NEGATIVE = -1e+30
FARAWAY = 1 << 30

def rotate(values, positions):
    rot_width = values.shape[-1]
    half_width = rot_width // 2
    inverse = jnp.exp(-jnp.log(10000.0) * (2.0 * jnp.arange(half_width, dtype=jnp.float32) / rot_width))
    angles = positions.astype(jnp.float32)[:, None] * inverse[None, :]
    cosine = jnp.cos(angles)[:, None, :]
    sine_table = jnp.sin(angles)[:, None, :]
    first_half = values[..., :half_width]
    second = values[..., half_width:]
    return jnp.concatenate([first_half * cosine - second * sine_table, second * cosine + first_half * sine_table], axis=-1)

def connect(streams, static, dynamic):
    widened = streams.astype(jnp.float32)
    products = jnp.einsum('tsd,dk->tsk', widened, dynamic.astype(jnp.float32), precision=lax.Precision.HIGHEST)
    stream_rms = jnp.sqrt(lax.optimization_barrier(jnp.mean(widened * widened, axis=2)) + EPS)
    weights = static[None] + jnp.tanh(products / stream_rms[:, :, None])
    mixture = lax.optimization_barrier(jnp.sum(weights[:, :, 0:1] * widened, axis=1))
    center = lax.optimization_barrier(jnp.mean(mixture, axis=1, keepdims=True))
    spread = lax.optimization_barrier(jnp.mean(mixture * mixture, axis=1, keepdims=True)) - center * center
    normed = ((mixture - center) / jnp.sqrt(spread + EPS)).astype(jnp.bfloat16)
    return (weights, widened, normed)

def blend(weights, widened, branch):
    stream_count = widened.shape[1]
    outputs = []
    for target in range(stream_count):
        carried = lax.optimization_barrier(jnp.sum(weights[:, :, 1 + target][:, :, None] * widened, axis=1))
        outputs.append(carried + weights[:, target, stream_count + 1][:, None] * branch)
    return jnp.stack(outputs, axis=1).astype(jnp.bfloat16)

def grouped_sum(left, right, groups):
    group_width = left.shape[1] // groups

    def add_group(summed, group_index):
        part_left = lax.dynamic_slice_in_dim(left, group_index * group_width, group_width, 1)
        part_right = lax.dynamic_slice_in_dim(right, group_index * group_width, group_width, 1)
        group_term = jnp.dot(part_left, part_right.T, preferred_element_type=jnp.float32).astype(jnp.bfloat16)
        group_term = lax.optimization_barrier(group_term)
        return (summed + group_term.astype(jnp.float32), None)
    zeros_init = jnp.zeros((left.shape[0], right.shape[0]), jnp.float32)
    summed, unused = lax.scan(add_group, zeros_init, jnp.arange(groups, dtype=jnp.int32))
    return summed

def reference(streams, lengths, cache, hc_static, hc_dynamic, w_qkv, w_out, w_gate_up, w_down):
    mix_attn, wide_attn, normed_attn = connect(streams, hc_static[0], hc_dynamic[0])
    projected = jnp.dot(normed_attn, w_qkv.reshape(D, HEADS * 3 * HD), preferred_element_type=jnp.float32)
    projected = projected.reshape(PROMPTS, STRETCH, HEADS, 3 * HD)
    stretch_offsets = jnp.arange(STRETCH, dtype=jnp.int32)
    cache_positions = jnp.arange(CACHE, dtype=jnp.int32)

    def per_prompt(bundle):
        proj_rows, length, cached = bundle
        positions = length + stretch_offsets
        queries = rotate(proj_rows[:, :, :HD], positions).astype(jnp.bfloat16)
        key_new = rotate(proj_rows[:, :, HD:2 * HD], positions).astype(jnp.bfloat16)
        value_new = proj_rows[:, :, 2 * HD:].astype(jnp.bfloat16)
        fresh_kv = jnp.concatenate([key_new, value_new], axis=2)
        key_pos = jnp.concatenate([jnp.where(cache_positions < length, cache_positions, FARAWAY), positions])
        allowed = key_pos[None, :] <= positions[:, None]

        def per_head(head_bundle):
            q_head, cache_head, fresh_head = head_bundle
            all_keys = jnp.concatenate([cache_head, fresh_head], axis=0)
            scores = jnp.dot(q_head, all_keys[:, :HD].T, preferred_element_type=jnp.float32) / math.sqrt(HD)
            scores = jnp.where(allowed, scores, NEGATIVE)
            row_max = lax.optimization_barrier(jnp.max(scores, axis=1, keepdims=True))
            unnormed = jnp.where(allowed, jnp.exp(scores - row_max), 0.0)
            denominator = lax.optimization_barrier(jnp.sum(unnormed, axis=1, keepdims=True))
            return (jnp.dot(unnormed.astype(jnp.bfloat16), all_keys[:, HD:], preferred_element_type=jnp.float32) / denominator).astype(jnp.bfloat16)
        attended_heads = lax.map(per_head, (jnp.transpose(queries, (1, 0, 2)), cached, jnp.transpose(fresh_kv, (1, 0, 2))))
        return (jnp.transpose(attended_heads, (1, 0, 2)).reshape(STRETCH, HEADS * HD), fresh_kv)
    attended, fresh_all = lax.map(per_prompt, (projected, lengths, cache))
    attended = attended.reshape(TOKENS, HEADS * HD)
    attn_branch = grouped_sum(attended, w_out, N_COL)
    streams_mid = blend(mix_attn, wide_attn, attn_branch)
    mix_ffn, wide_ffn, normed_ffn = connect(streams_mid, hc_static[1], hc_dynamic[1])
    gate = jnp.dot(normed_ffn, w_gate_up[:, 0, :], preferred_element_type=jnp.float32)
    up_proj = jnp.dot(normed_ffn, w_gate_up[:, 1, :], preferred_element_type=jnp.float32)
    hidden = (jax.nn.silu(gate) * up_proj).astype(jnp.bfloat16)
    ffn_branch = grouped_sum(hidden, w_down, N_COL)
    new_streams = blend(mix_ffn, wide_ffn, ffn_branch)
    decode_cache = jnp.transpose(cache.reshape(PROMPTS, HEADS, N_REP, CACHE_DEV, 2 * HD), (0, 2, 1, 3, 4))
    decode_new = fresh_all.reshape(PROMPTS, N_COL, N_REP, TOK_DEV, HEADS, 2 * HD)
    decode_new = jnp.transpose(decode_new, (0, 2, 4, 1, 3, 5)).reshape(PROMPTS, N_REP, HEADS, N_COL * TOK_DEV, 2 * HD)
    return (new_streams, decode_cache, decode_new)
```

```python
import functools
import math

import jax
import jax.numpy as jnp
from jax import lax
from jax.experimental import pallas as pl
from jax.experimental.pallas import tpu as pltpu
from jax.sharding import Mesh
from jax.sharding import PartitionSpec as P

EPS = 1e-05
NEGATIVE = -1e30
MESH = pl.DeviceIdType.MESH
ROW = ("zl", "y")
COL = ("x", "zh")
NX = 4
NZ = 4
BF = jnp.bfloat16
F32 = jnp.float32
VMEM_ALL = pl.BlockSpec(memory_space=pltpu.VMEM)
ANY = pl.BlockSpec(memory_space=pl.ANY)


def rope_tables(positions, rot_width):
    half_width = rot_width // 2
    inverse = jnp.exp(
        -jnp.log(10000.0) * (2.0 * jnp.arange(half_width, dtype=F32) / rot_width)
    )
    angles = positions.astype(F32)[:, None] * inverse[None, :]
    return jnp.cos(angles), jnp.sin(angles)


def rotate(values, cosine, sine):
    half_width = values.shape[-1] // 2
    first, second = values[:, :half_width], values[:, half_width:]
    return jnp.concatenate(
        [first * cosine - second * sine, second * cosine + first * sine], axis=-1
    )


def connect(streams, static, dynamic):
    widened = streams.astype(F32)
    products = jnp.einsum("tsd,dk->tsk", streams, dynamic, preferred_element_type=F32)
    stream_rms = jnp.sqrt(jnp.mean(widened * widened, axis=2) + EPS)
    weights = static[None] + jnp.tanh(products / stream_rms[:, :, None])
    mixture = jnp.sum(weights[:, :, 0:1] * widened, axis=1)
    center = jnp.mean(mixture, axis=1, keepdims=True)
    spread = jnp.mean(mixture * mixture, axis=1, keepdims=True) - center * center
    normed = ((mixture - center) / jnp.sqrt(spread + EPS)).astype(BF)
    return (weights, widened, normed)


def blend(weights, widened, branch):
    stream_count = widened.shape[1]
    outputs = []
    for target in range(stream_count):
        carried = jnp.sum(weights[:, :, 1 + target][:, :, None] * widened, axis=1)
        outputs.append(carried + weights[:, target, stream_count + 1][:, None] * branch)
    return jnp.stack(outputs, axis=1).astype(BF)


def around():
    x, z = lax.axis_index("x"), lax.axis_index("zh")
    return (
        x,
        z,
        lax.rem(x + 1, NX),
        lax.rem(x + NX - 1, NX),
        lax.rem(z + 1, NZ),
        lax.rem(z + NZ - 1, NZ),
    )


def greet(places):
    barrier = pltpu.get_barrier_semaphore()
    for place in places:
        pl.semaphore_signal(barrier, inc=1, device_id=place, device_id_type=MESH)
    pl.semaphore_wait(barrier, len(places))


def gather_kernel(t_ref, o_ref, send_sem, recv_sem, own_sem):
    x, z, xr, xl, zu, zd = around()
    right, left, up, down = {"x": xr}, {"x": xl}, {"zh": zu}, {"zh": zd}
    x2, z2 = lax.rem(x + 2, NX), lax.rem(z + 2, NZ)
    half = t_ref.shape[0] // 2
    top, low = pl.ds(0, half), pl.ds(half, half)
    whole = pl.ds(0, 2 * half)
    greet((right, left, up, down))

    def copy(kind, src, slot, rows, place):
        return pltpu.make_async_remote_copy(
            src_ref=src.at[rows],
            dst_ref=o_ref.at[slot, rows],
            send_sem=send_sem.at[kind],
            recv_sem=recv_sem.at[kind],
            device_id=place,
            device_id_type=MESH,
        )

    started = []

    def start(*given):
        made = copy(*given)
        made.start()
        started.append(made)

    mine = x * NZ + z

    def arrived(kind, slot, rows, place):
        copy(kind, t_ref, slot, rows, place).wait_recv()

    own = pltpu.make_async_copy(t_ref, o_ref.at[mine], own_sem)
    start(0, t_ref, mine, whole, up)
    start(1, t_ref, mine, whole, down)
    start(4, t_ref, mine, whole, right)
    start(5, t_ref, mine, whole, left)
    own.start()
    zs = (z, zd, zu, z2)
    below, above = x * NZ + zd, x * NZ + zu
    arrived(0, mine, whole, up)
    start(2, o_ref.at[below], below, top, up)
    start(8, o_ref.at[below], below, whole, right)
    start(9, o_ref.at[below], below, whole, left)
    arrived(1, mine, whole, down)
    start(3, o_ref.at[above], above, low, down)
    start(12, o_ref.at[above], above, whole, right)
    start(13, o_ref.at[above], above, whole, left)

    def relay(j):
        from_left, from_right = xl * NZ + zs[j], xr * NZ + zs[j]
        arrived(4 + 4 * j, mine, whole, right)
        start(6 + 4 * j, o_ref.at[from_left], from_left, top, right)
        arrived(5 + 4 * j, mine, whole, left)
        start(7 + 4 * j, o_ref.at[from_right], from_right, low, left)

    relay(0)
    far = x * NZ + z2
    arrived(2, mine, top, up)
    arrived(3, mine, low, down)
    start(16, o_ref.at[far], far, whole, right)
    start(17, o_ref.at[far], far, whole, left)
    relay(1)
    relay(2)
    relay(3)
    for j in range(4):
        arrived(6 + 4 * j, mine, top, right)
        arrived(7 + 4 * j, mine, low, left)
    own.wait()
    for made in started:
        made.wait_send()


def gather_tokens(block, number):
    rows, width = block.shape
    return pl.pallas_call(
        gather_kernel,
        out_shape=jax.ShapeDtypeStruct((NX * NZ, rows, width), BF),
        in_specs=[VMEM_ALL],
        out_specs=VMEM_ALL,
        scratch_shapes=[
            pltpu.SemaphoreType.DMA((20,)),
            pltpu.SemaphoreType.DMA((20,)),
            pltpu.SemaphoreType.DMA,
        ],
        compiler_params=pltpu.CompilerParams(
            collective_id=number, has_side_effects=True, vmem_limit_bytes=48 << 20
        ),
        name="gather_tokens",
    )(block)


def scatter_kernel(p_ref, o_ref, xin, xsum, tin, total, tsum, send_sem, recv_sem):
    x, z, xr, xl, zu, zd = around()
    right, left, up, down = {"x": xr}, {"x": xl}, {"zh": zu}, {"zh": zd}
    x2, z2 = lax.rem(x + 2, NX), lax.rem(z + 2, NZ)
    half = p_ref.shape[1] // 2
    top, low = pl.ds(0, half), pl.ds(half, half)
    greet((right, left, up, down))
    started = []

    def copy(kind, src, dst, place):
        return pltpu.make_async_remote_copy(
            src_ref=src,
            dst_ref=dst,
            send_sem=send_sem.at[kind],
            recv_sem=recv_sem.at[kind],
            device_id=place,
            device_id_type=MESH,
        )

    def start(*given):
        made = copy(*given)
        made.start()
        started.append(made)

    def arrived(kind, ref, place):
        copy(kind, ref, ref, place).wait_recv()

    zs = (z2, zu, zd, z)
    for j in range(4):
        far = x2 * NZ + zs[j]
        start(6 * j, p_ref.at[far, top], xin.at[j, 0], right)
        start(6 * j + 1, p_ref.at[far, low], xin.at[j, 1], left)
    for j in range(4):
        start(6 * j + 2, p_ref.at[xr * NZ + zs[j], low], xin.at[j, 2], right)
        start(6 * j + 3, p_ref.at[xl * NZ + zs[j], top], xin.at[j, 3], left)

    def wide(ref):
        return ref[...].astype(F32)

    for j in range(4):
        arrived(6 * j, xin.at[j, 0], right)
        xsum[j, 0] = (wide(p_ref.at[xr * NZ + zs[j], top]) + wide(xin.at[j, 0])).astype(BF)
        start(6 * j + 4, xsum.at[j, 0], xin.at[j, 4], right)
        arrived(6 * j + 1, xin.at[j, 1], left)
        xsum[j, 1] = (wide(p_ref.at[xl * NZ + zs[j], low]) + wide(xin.at[j, 1])).astype(BF)
        start(6 * j + 5, xsum.at[j, 1], xin.at[j, 5], left)

    def finish_x(j):
        for kind, place in ((2, right), (3, left), (4, right), (5, left)):
            arrived(6 * j + kind, xin.at[j, kind], place)
        here = x * NZ + zs[j]
        a = wide(p_ref.at[here, top]) + wide(xin.at[j, 4]) + wide(xin.at[j, 3])
        b = wide(p_ref.at[here, low]) + wide(xin.at[j, 2]) + wide(xin.at[j, 5])
        return a, b

    base = 24
    a, b = finish_x(0)
    total[0, 0], total[0, 1] = a.astype(BF), b.astype(BF)
    start(base, total.at[0, 0], tin.at[0], up)
    start(base + 1, total.at[0, 1], tin.at[1], down)
    a, b = finish_x(1)
    total[1, 1] = b.astype(BF)
    start(base + 2, total.at[1, 1], tin.at[2], up)
    arrived(base, tin.at[0], up)
    tsum[0] = (a + wide(tin.at[0])).astype(BF)
    start(base + 4, tsum.at[0], tin.at[4], up)
    a, b = finish_x(2)
    total[2, 0] = a.astype(BF)
    start(base + 3, total.at[2, 0], tin.at[3], down)
    arrived(base + 1, tin.at[1], down)
    tsum[1] = (b + wide(tin.at[1])).astype(BF)
    start(base + 5, tsum.at[1], tin.at[5], down)
    a, b = finish_x(3)
    for kind, place in ((2, up), (3, down), (4, up), (5, down)):
        arrived(base + kind, tin.at[kind], place)
    o_ref[top] = a + wide(tin.at[4]) + wide(tin.at[3])
    o_ref[low] = b + wide(tin.at[2]) + wide(tin.at[5])
    for made in started:
        made.wait_send()


def scatter_sum(partial, number):
    blocks, rows, width = partial.shape
    half = rows // 2
    return pl.pallas_call(
        scatter_kernel,
        out_shape=jax.ShapeDtypeStruct((rows, width), F32),
        in_specs=[VMEM_ALL],
        out_specs=VMEM_ALL,
        scratch_shapes=[
            pltpu.VMEM((4, 6, half, width), BF),
            pltpu.VMEM((4, 2, half, width), BF),
            pltpu.VMEM((6, half, width), BF),
            pltpu.VMEM((3, 2, half, width), BF),
            pltpu.VMEM((2, half, width), BF),
            pltpu.SemaphoreType.DMA((30,)),
            pltpu.SemaphoreType.DMA((30,)),
        ],
        compiler_params=pltpu.CompilerParams(
            collective_id=number, has_side_effects=True, vmem_limit_bytes=48 << 20
        ),
        name="scatter_sum",
    )(partial)


def decode_kernel(c_ref, f_ref, dc_ref, dn_ref, send_sem, recv_sem):
    x, z, e = lax.axis_index("x"), lax.axis_index("zh"), lax.axis_index("core")
    col = x * NZ + z
    count = NX * NZ
    per = dc_ref.shape[1]
    crows, frows = dc_ref.shape[2], dn_ref.shape[2]
    to_core, slot = col // per, lax.rem(col, per)
    barrier = pltpu.get_barrier_semaphore()

    def at(c, core):
        return {"x": c // NZ, "zh": lax.rem(c, NZ), "core": core}

    for s in range(per):
        source = e * per + lax.rem(slot + s, per)
        for core in range(2):

            @pl.when(jnp.logical_not(jnp.logical_and(source == col, e == core)))
            def _():
                pl.semaphore_signal(
                    barrier, inc=1, device_id=at(source, core), device_id_type=MESH
                )

    stays = (to_core == e).astype(jnp.int32)
    pl.semaphore_wait(barrier, count - stays)

    def pieces(c):
        return (
            (c_ref.at[pl.ds(pl.multiple_of(c * crows, crows), crows)], dc_ref.at[e, slot]),
            (f_ref.at[pl.ds(pl.multiple_of(c * frows, frows), frows)], dn_ref.at[e, slot]),
        )

    def remote(s, kind):
        c = lax.rem(col + s, count)
        src, dst = pieces(c)[kind]
        return pltpu.make_async_remote_copy(
            src_ref=src,
            dst_ref=dst,
            send_sem=send_sem.at[kind, s],
            recv_sem=recv_sem.at[kind, e, slot],
            device_id=at(c, to_core),
            device_id_type=MESH,
        )

    def local(kind):
        src, dst = pieces(col)[kind]
        return pltpu.make_async_copy(src, dst, send_sem.at[kind, 0])

    for s in range(1, count):
        for kind in range(2):
            remote(s, kind).start()
    for kind in range(2):

        @pl.when(to_core == e)
        def _():
            local(kind).start()

        @pl.when(to_core != e)
        def _():
            remote(0, kind).start()

    for core in range(2):
        for i in range(per):
            for kind, ref in ((0, dc_ref), (1, dn_ref)):

                @pl.when(jnp.logical_not(jnp.logical_and(core == e, e * per + i == col)))
                def _():
                    pltpu.make_async_remote_copy(
                        src_ref=ref.at[core, i],
                        dst_ref=ref.at[core, i],
                        send_sem=send_sem.at[kind, 0],
                        recv_sem=recv_sem.at[kind, core, i],
                        device_id=at(col, 1 - e),
                        device_id_type=MESH,
                    ).wait_recv()

    for s in range(1, count):
        for kind in range(2):
            remote(s, kind).wait_send()
    for kind in range(2):

        @pl.when(to_core == e)
        def _():
            local(kind).wait()

        @pl.when(to_core != e)
        def _():
            remote(0, kind).wait_send()


def decode_exchange(cache, fresh, number):
    count = NX * NZ
    per = count // 2
    (crows, width), frows = cache.shape, fresh.shape[0]
    return pl.pallas_call(
        decode_kernel,
        out_shape=(
            jax.ShapeDtypeStruct((2, per, crows // count, width), BF),
            jax.ShapeDtypeStruct((2, per, frows // count, width), BF),
        ),
        in_specs=[ANY, ANY],
        out_specs=(ANY, ANY),
        scratch_shapes=[
            pltpu.SemaphoreType.DMA((2, count)),
            pltpu.SemaphoreType.DMA((2, 2, per)),
        ],
        compiler_params=pltpu.CompilerParams(collective_id=number, has_side_effects=True),
        name="decode_exchange",
    )(cache, fresh)


SUB = 256
KEYS = 512


def attend_kernel(meta, q_ref, co_ref, cx_ref, fo_ref, fx_ref, o_ref, m_ref, l_ref, acc_ref):
    hd = q_ref.shape[1]
    subs = q_ref.shape[0] // SUB
    gain = 1.0 / (math.sqrt(hd) * math.log(2.0))
    length, rep = meta[0], meta[1]
    m_ref[...] = jnp.full_like(m_ref, NEGATIVE)
    l_ref[...] = jnp.zeros_like(l_ref)
    acc_ref[...] = jnp.zeros_like(acc_ref)

    def absorb(sub, keys, values, allowed):
        rows = pl.ds(sub * SUB, SUB)
        scores = lax.dot_general(
            q_ref[rows], keys, (((1,), (1,)), ((), ())), preferred_element_type=F32
        )
        if allowed is not None:
            scores = jnp.where(allowed, scores, NEGATIVE)
        before = m_ref[rows]
        newest = jnp.maximum(before, jnp.max(scores, axis=1, keepdims=True))
        factor = jnp.exp2((before - newest) * gain)
        probs = jnp.exp2((scores - newest[:, :1]) * gain)
        if allowed is not None:
            probs = jnp.where(allowed, probs, 0.0)
        m_ref[rows] = newest
        l_ref[rows] = l_ref[rows] * factor + jnp.sum(probs, axis=1, keepdims=True)
        acc_ref[rows] = acc_ref[rows] * factor + jnp.dot(
            probs.astype(BF), values, preferred_element_type=F32
        )

    def cached(ref, base):
        def one(number, unused):
            first = base + number * KEYS
            rows = pl.ds(pl.multiple_of(number * KEYS, KEYS), KEYS)

            @pl.when(first + KEYS <= length)
            def _():
                for sub in range(subs):
                    absorb(sub, ref[rows, :hd], ref[rows, hd:], None)

            @pl.when(jnp.logical_and(first < length, first + KEYS > length))
            def _():
                place = first + lax.broadcasted_iota(jnp.int32, (SUB, KEYS), 1)
                for sub in range(subs):
                    absorb(sub, ref[rows, :hd], ref[rows, hd:], place < length)

            return unused

        lax.fori_loop(0, ref.shape[0] // KEYS, one, 0)

    reach = co_ref.shape[0]
    cached(co_ref, rep * reach)
    cached(cx_ref, (1 - rep) * reach)
    tok = meta_tok(q_ref.shape[0])
    row = lax.broadcasted_iota(jnp.int32, (SUB, SUB), 0)
    column = lax.broadcasted_iota(jnp.int32, (SUB, SUB), 1)
    own_ok = column <= row
    other_ok = column // tok < row // tok + rep
    for number in range(subs):
        rows = pl.ds(number * SUB, SUB)
        for ref, allowed in ((fo_ref, own_ok), (fx_ref, other_ok)):
            for sub in range(number, subs):
                absorb(
                    sub, ref[rows, :hd], ref[rows, hd:], allowed if sub == number else None
                )
    o_ref[...] = (acc_ref[...] / l_ref[...]).astype(o_ref.dtype)


def meta_tok(rows):
    return rows // (NX * NZ)


def attend(meta, queries, cache_own, cache_other, fresh_own, fresh_other):
    rows, hd = queries.shape
    return pl.pallas_call(
        attend_kernel,
        out_shape=jax.ShapeDtypeStruct((rows, hd), BF),
        in_specs=[pl.BlockSpec(memory_space=pltpu.SMEM)] + [VMEM_ALL] * 5,
        out_specs=VMEM_ALL,
        scratch_shapes=[pltpu.VMEM((rows, hd), F32)] * 3,
        compiler_params=pltpu.CompilerParams(vmem_limit_bytes=48 << 20),
        cost_estimate=pl.CostEstimate(
            flops=4 * rows * hd * 5120,
            bytes_accessed=4 << 20,
            transcendentals=rows * 5120,
        ),
        name="attend",
    )(meta, queries, cache_own, cache_other, fresh_own, fresh_other)


def gather_rows(weight, rep_index):
    half = weight.shape[0] // 2
    mine = lax.dynamic_slice_in_dim(weight, rep_index * half, half, 0)
    return lax.all_gather(mine, ROW + ("core",), axis=0, tiled=True)


def swap(value):
    return lax.ppermute(value, "core", [(0, 1), (1, 0)])


def on_device(streams, lengths, cache, hc_static, hc_dynamic, w_qkv, w_out, w_gate_up, w_down):
    rep_count = 2
    col_count = NX * NZ
    rep_index = lax.axis_index("core")
    tok_dev, stream_count, width = streams.shape
    tok_rep = tok_dev * col_count
    head_dim = w_qkv.shape[2] // 3
    length = lengths[0]
    cache = cache[0, 0]
    cache_other = swap(cache)
    mix_attn, wide_attn, normed_attn = connect(streams, hc_static[0], hc_dynamic[0])
    input_attn = gather_tokens(normed_attn, 0).reshape(tok_rep, width)
    qkv_rows = gather_rows(w_qkv[:, 0, :], rep_index)
    projected = jnp.dot(input_attn, qkv_rows, preferred_element_type=F32)
    row_ids = jnp.arange(tok_rep, dtype=jnp.int32)
    stretch_ids = (row_ids // tok_dev * rep_count + rep_index) * tok_dev + row_ids % tok_dev
    cosine, sine = rope_tables(length + stretch_ids, head_dim)
    queries = rotate(projected[:, :head_dim], cosine, sine).astype(BF)
    key_new = rotate(projected[:, head_dim : 2 * head_dim], cosine, sine).astype(BF)
    value_new = projected[:, 2 * head_dim :].astype(BF)
    fresh = jnp.concatenate([key_new, value_new], axis=1)
    fresh_other = swap(fresh)
    meta = jnp.stack([length, rep_index])
    attended = attend(meta, queries, cache, cache_other, fresh, fresh_other)
    out_rows = gather_rows(w_out, rep_index)
    attn_partial = lax.dot_general(
        attended, out_rows, (((1,), (1,)), ((), ())), preferred_element_type=F32
    ).astype(BF)
    attn_branch = scatter_sum(attn_partial.reshape(col_count, tok_dev, width), 1)
    streams_mid = blend(mix_attn, wide_attn, attn_branch)
    mix_ffn, wide_ffn, normed_ffn = connect(streams_mid, hc_static[1], hc_dynamic[1])
    input_ffn = gather_tokens(normed_ffn, 2).reshape(tok_rep, width)
    gate_rows = gather_rows(w_gate_up, rep_index)
    down_rows = gather_rows(w_down, rep_index)
    gate_up = jnp.einsum("td,dkf->tkf", input_ffn, gate_rows, preferred_element_type=F32)
    hidden = (jax.nn.silu(gate_up[:, 0]) * gate_up[:, 1]).astype(BF)
    ffn_partial = lax.dot_general(
        hidden, down_rows, (((1,), (1,)), ((), ())), preferred_element_type=F32
    ).astype(BF)
    ffn_branch = scatter_sum(ffn_partial.reshape(col_count, tok_dev, width), 3)
    new_streams = blend(mix_ffn, wide_ffn, ffn_branch)
    decode_cache, decode_new = decode_exchange(cache, fresh, 4)
    return (new_streams, decode_cache[None], decode_new[None])


def solution(mesh):
    rows = mesh.devices.shape[0]
    fine = Mesh(
        mesh.devices.reshape((2, rows // 2, NX, NZ, 2)), ("zl", "y", "x", "zh", "core")
    )
    placed = (
        P(ROW + COL + ("core",), None, None),
        P(ROW),
        P(ROW, COL, "core", None),
        P(),
        P(),
        P(ROW, COL, None),
        P(ROW, COL),
        P(ROW, None, COL),
        P(ROW, COL),
    )
    return jax.shard_map(
        on_device,
        mesh=fine,
        in_specs=placed,
        out_specs=(
            P(ROW + COL + ("core",), None, None),
            P(ROW, None, "core", COL, None),
            P(ROW, None, "core", COL, None),
        ),
        check_vma=False,
    )
```

```python
import functools
import math

import jax
import jax.numpy as jnp
from jax import lax
from jax.experimental import pallas as pl
from jax.experimental.layout import Layout, with_layout_constraint
from jax.experimental.pallas import tpu as pltpu
from jax.sharding import Mesh
from jax.sharding import PartitionSpec as P

EPS = 1e-05
NEGATIVE = -1e30
MESH = pl.DeviceIdType.MESH
ROW = ("zl", "y")
COL = ("x", "zh")
NX = 4
NZ = 4
BF = jnp.bfloat16
F32 = jnp.float32
VMEM_ALL = pl.BlockSpec(memory_space=pltpu.VMEM)
ANY = pl.BlockSpec(memory_space=pl.ANY)


def rope_tables(positions, rot_width):
    half_width = rot_width // 2
    inverse = jnp.exp(
        -jnp.log(10000.0) * (2.0 * jnp.arange(half_width, dtype=F32) / rot_width)
    )
    angles = positions.astype(F32)[:, None] * inverse[None, :]
    return jnp.cos(angles), jnp.sin(angles)


def rotate(values, cosine, sine):
    half_width = values.shape[-1] // 2
    first, second = values[:, :half_width], values[:, half_width:]
    return jnp.concatenate(
        [first * cosine - second * sine, second * cosine + first * sine], axis=-1
    )


def connect(streams, static, dynamic):
    widened = streams.astype(F32)
    products = jnp.einsum("std,dk->stk", streams, dynamic, preferred_element_type=F32)
    stream_rms = jnp.sqrt(jnp.mean(widened * widened, axis=2) + EPS)
    weights = static[:, None] + jnp.tanh(products / stream_rms[:, :, None])
    mixture = jnp.sum(weights[:, :, 0:1] * widened, axis=0)
    center = jnp.mean(mixture, axis=1, keepdims=True)
    spread = jnp.mean(mixture * mixture, axis=1, keepdims=True) - center * center
    normed = ((mixture - center) / jnp.sqrt(spread + EPS)).astype(BF)
    return (weights, normed)


def blend(weights, streams, branch):
    stream_count = streams.shape[0]
    widened = streams.astype(F32)
    outputs = []
    for target in range(stream_count):
        carried = jnp.sum(weights[:, :, 1 + target][:, :, None] * widened, axis=0)
        outputs.append(carried + weights[target, :, stream_count + 1][:, None] * branch)
    return jnp.stack(outputs, axis=0).astype(BF)


def around():
    x, z = lax.axis_index("x"), lax.axis_index("zh")
    return (
        x,
        z,
        lax.rem(x + 1, NX),
        lax.rem(x + NX - 1, NX),
        lax.rem(z + 1, NZ),
        lax.rem(z + NZ - 1, NZ),
    )


def greet(places):
    barrier = pltpu.get_barrier_semaphore()
    for place in places:
        pl.semaphore_signal(barrier, inc=1, device_id=place, device_id_type=MESH)
    pl.semaphore_wait(barrier, len(places))


def gather_kernel(t_ref, o_ref, send_sem, recv_sem, own_sem):
    x, z, xr, xl, zu, zd = around()
    right, left, up, down = {"x": xr}, {"x": xl}, {"zh": zu}, {"zh": zd}
    x2, z2 = lax.rem(x + 2, NX), lax.rem(z + 2, NZ)
    half = t_ref.shape[0] // 2
    top, low = pl.ds(0, half), pl.ds(half, half)
    whole = pl.ds(0, 2 * half)
    greet((right, left, up, down))

    def copy(kind, src, slot, rows, place):
        return pltpu.make_async_remote_copy(
            src_ref=src.at[rows],
            dst_ref=o_ref.at[slot, rows],
            send_sem=send_sem.at[kind],
            recv_sem=recv_sem.at[kind],
            device_id=place,
            device_id_type=MESH,
        )

    started = []

    def start(*given):
        made = copy(*given)
        made.start()
        started.append(made)

    mine = x * NZ + z

    def arrived(kind, slot, rows, place):
        copy(kind, t_ref, slot, rows, place).wait_recv()

    own = pltpu.make_async_copy(t_ref, o_ref.at[mine], own_sem)
    start(0, t_ref, mine, whole, up)
    start(1, t_ref, mine, whole, down)
    start(4, t_ref, mine, whole, right)
    start(5, t_ref, mine, whole, left)
    own.start()
    zs = (z, zd, zu, z2)
    below, above = x * NZ + zd, x * NZ + zu
    arrived(0, mine, whole, up)
    start(2, o_ref.at[below], below, top, up)
    start(8, o_ref.at[below], below, whole, right)
    start(9, o_ref.at[below], below, whole, left)
    arrived(1, mine, whole, down)
    start(3, o_ref.at[above], above, low, down)
    start(12, o_ref.at[above], above, whole, right)
    start(13, o_ref.at[above], above, whole, left)

    def relay(j):
        from_left, from_right = xl * NZ + zs[j], xr * NZ + zs[j]
        arrived(4 + 4 * j, mine, whole, right)
        start(6 + 4 * j, o_ref.at[from_left], from_left, top, right)
        arrived(5 + 4 * j, mine, whole, left)
        start(7 + 4 * j, o_ref.at[from_right], from_right, low, left)

    relay(0)
    far = x * NZ + z2
    arrived(2, mine, top, up)
    arrived(3, mine, low, down)
    start(16, o_ref.at[far], far, whole, right)
    start(17, o_ref.at[far], far, whole, left)
    relay(1)
    relay(2)
    relay(3)
    for j in range(4):
        arrived(6 + 4 * j, mine, top, right)
        arrived(7 + 4 * j, mine, low, left)
    own.wait()
    for made in started:
        made.wait_send()


def gather_tokens(block, number):
    rows, width = block.shape
    return pl.pallas_call(
        gather_kernel,
        out_shape=jax.ShapeDtypeStruct((NX * NZ, rows, width), BF),
        in_specs=[VMEM_ALL],
        out_specs=VMEM_ALL,
        scratch_shapes=[
            pltpu.SemaphoreType.DMA((20,)),
            pltpu.SemaphoreType.DMA((20,)),
            pltpu.SemaphoreType.DMA,
        ],
        compiler_params=pltpu.CompilerParams(
            collective_id=number, has_side_effects=True, vmem_limit_bytes=48 << 20
        ),
        name="gather_tokens",
    )(block)


def scatter_kernel(p_ref, o_ref, xin, xsum, tin, total, tsum, send_sem, recv_sem):
    x, z, xr, xl, zu, zd = around()
    right, left, up, down = {"x": xr}, {"x": xl}, {"zh": zu}, {"zh": zd}
    x2, z2 = lax.rem(x + 2, NX), lax.rem(z + 2, NZ)
    half = p_ref.shape[1] // 2
    top, low = pl.ds(0, half), pl.ds(half, half)
    greet((right, left, up, down))
    started = []

    def copy(kind, src, dst, place):
        return pltpu.make_async_remote_copy(
            src_ref=src,
            dst_ref=dst,
            send_sem=send_sem.at[kind],
            recv_sem=recv_sem.at[kind],
            device_id=place,
            device_id_type=MESH,
        )

    def start(*given):
        made = copy(*given)
        made.start()
        started.append(made)

    def arrived(kind, ref, place):
        copy(kind, ref, ref, place).wait_recv()

    zs = (z2, zu, zd, z)
    for j in range(4):
        far = x2 * NZ + zs[j]
        start(6 * j, p_ref.at[far, top], xin.at[j, 0], right)
        start(6 * j + 1, p_ref.at[far, low], xin.at[j, 1], left)
    for j in range(4):
        start(6 * j + 2, p_ref.at[xr * NZ + zs[j], low], xin.at[j, 2], right)
        start(6 * j + 3, p_ref.at[xl * NZ + zs[j], top], xin.at[j, 3], left)

    def wide(ref):
        return ref[...].astype(F32)

    for j in range(4):
        arrived(6 * j, xin.at[j, 0], right)
        xsum[j, 0] = (wide(p_ref.at[xr * NZ + zs[j], top]) + wide(xin.at[j, 0])).astype(BF)
        start(6 * j + 4, xsum.at[j, 0], xin.at[j, 4], right)
        arrived(6 * j + 1, xin.at[j, 1], left)
        xsum[j, 1] = (wide(p_ref.at[xl * NZ + zs[j], low]) + wide(xin.at[j, 1])).astype(BF)
        start(6 * j + 5, xsum.at[j, 1], xin.at[j, 5], left)

    def finish_x(j):
        for kind, place in ((2, right), (3, left), (4, right), (5, left)):
            arrived(6 * j + kind, xin.at[j, kind], place)
        here = x * NZ + zs[j]
        a = wide(p_ref.at[here, top]) + wide(xin.at[j, 4]) + wide(xin.at[j, 3])
        b = wide(p_ref.at[here, low]) + wide(xin.at[j, 2]) + wide(xin.at[j, 5])
        return a, b

    base = 24
    a, b = finish_x(0)
    total[0, 0], total[0, 1] = a.astype(BF), b.astype(BF)
    start(base, total.at[0, 0], tin.at[0], up)
    start(base + 1, total.at[0, 1], tin.at[1], down)
    a, b = finish_x(1)
    total[1, 1] = b.astype(BF)
    start(base + 2, total.at[1, 1], tin.at[2], up)
    arrived(base, tin.at[0], up)
    tsum[0] = (a + wide(tin.at[0])).astype(BF)
    start(base + 4, tsum.at[0], tin.at[4], up)
    a, b = finish_x(2)
    total[2, 0] = a.astype(BF)
    start(base + 3, total.at[2, 0], tin.at[3], down)
    arrived(base + 1, tin.at[1], down)
    tsum[1] = (b + wide(tin.at[1])).astype(BF)
    start(base + 5, tsum.at[1], tin.at[5], down)
    a, b = finish_x(3)
    for kind, place in ((2, up), (3, down), (4, up), (5, down)):
        arrived(base + kind, tin.at[kind], place)
    o_ref[top] = a + wide(tin.at[4]) + wide(tin.at[3])
    o_ref[low] = b + wide(tin.at[2]) + wide(tin.at[5])
    for made in started:
        made.wait_send()


def scatter_sum(partial, number):
    blocks, rows, width = partial.shape
    half = rows // 2
    return pl.pallas_call(
        scatter_kernel,
        out_shape=jax.ShapeDtypeStruct((rows, width), F32),
        in_specs=[VMEM_ALL],
        out_specs=VMEM_ALL,
        scratch_shapes=[
            pltpu.VMEM((4, 6, half, width), BF),
            pltpu.VMEM((4, 2, half, width), BF),
            pltpu.VMEM((6, half, width), BF),
            pltpu.VMEM((3, 2, half, width), BF),
            pltpu.VMEM((2, half, width), BF),
            pltpu.SemaphoreType.DMA((30,)),
            pltpu.SemaphoreType.DMA((30,)),
        ],
        compiler_params=pltpu.CompilerParams(
            collective_id=number, has_side_effects=True, vmem_limit_bytes=48 << 20
        ),
        name="scatter_sum",
    )(partial)


def decode_copies(c_ref, f_ref, dc_ref, dn_ref, send_sem, recv_sem):
    x, z, e = lax.axis_index("x"), lax.axis_index("zh"), lax.axis_index("core")
    col = x * NZ + z
    count = NX * NZ
    per = dc_ref.shape[1]
    crows, frows = dc_ref.shape[2], dn_ref.shape[2]
    to_core, slot = col // per, lax.rem(col, per)
    barrier = pltpu.get_barrier_semaphore()

    def at(c, core):
        return {"x": c // NZ, "zh": lax.rem(c, NZ), "core": core}

    for s in range(per):
        source = e * per + lax.rem(slot + s, per)
        for core in range(2):

            @pl.when(jnp.logical_not(jnp.logical_and(source == col, e == core)))
            def _():
                pl.semaphore_signal(
                    barrier, inc=1, device_id=at(source, core), device_id_type=MESH
                )

    stays = (to_core == e).astype(jnp.int32)
    pl.semaphore_wait(barrier, count - stays)

    def pieces(c):
        return (
            (c_ref.at[pl.ds(pl.multiple_of(c * crows, crows), crows)], dc_ref.at[e, slot]),
            (f_ref.at[pl.ds(pl.multiple_of(c * frows, frows), frows)], dn_ref.at[e, slot]),
        )

    def remote(s, kind):
        c = lax.rem(col + s, count)
        src, dst = pieces(c)[kind]
        return pltpu.make_async_remote_copy(
            src_ref=src,
            dst_ref=dst,
            send_sem=send_sem.at[kind, s],
            recv_sem=recv_sem.at[kind, e, slot],
            device_id=at(c, to_core),
            device_id_type=MESH,
        )

    def local(kind):
        src, dst = pieces(col)[kind]
        return pltpu.make_async_copy(src, dst, send_sem.at[kind, 0])

    for s in range(1, count):
        for kind in range(2):
            remote(s, kind).start()
    for kind in range(2):

        @pl.when(to_core == e)
        def _():
            local(kind).start()

        @pl.when(to_core != e)
        def _():
            remote(0, kind).start()

    yield
    for core in range(2):
        for i in range(per):
            for kind, ref in ((0, dc_ref), (1, dn_ref)):

                @pl.when(jnp.logical_not(jnp.logical_and(core == e, e * per + i == col)))
                def _():
                    pltpu.make_async_remote_copy(
                        src_ref=ref.at[core, i],
                        dst_ref=ref.at[core, i],
                        send_sem=send_sem.at[kind, 0],
                        recv_sem=recv_sem.at[kind, core, i],
                        device_id=at(col, 1 - e),
                        device_id_type=MESH,
                    ).wait_recv()

    for s in range(1, count):
        for kind in range(2):
            remote(s, kind).wait_send()
    for kind in range(2):

        @pl.when(to_core == e)
        def _():
            local(kind).wait()

        @pl.when(to_core != e)
        def _():
            remote(0, kind).wait_send()


SUB = 256
KEYS = 512


def attend_kernel(
    meta, q_ref, co_ref, cx_ref, fo_ref, fx_ref, o_ref, dc_ref, dn_ref,
    m_ref, l_ref, acc_ref, send_sem, recv_sem,
):
    hd = q_ref.shape[1]
    subs = q_ref.shape[0] // SUB
    gain = 1.0 / (math.sqrt(hd) * math.log(2.0))
    length, rep = meta[0], lax.axis_index("core")
    copies = decode_copies(co_ref, fo_ref, dc_ref, dn_ref, send_sem, recv_sem)
    next(copies)
    m_ref[...] = jnp.full_like(m_ref, NEGATIVE)
    l_ref[...] = jnp.zeros_like(l_ref)
    acc_ref[...] = jnp.zeros_like(acc_ref)

    def absorb(sub, keys, values, allowed):
        rows = pl.ds(sub * SUB, SUB)
        scores = lax.dot_general(
            q_ref[rows], keys, (((1,), (1,)), ((), ())), preferred_element_type=F32
        )
        if allowed is not None:
            scores = jnp.where(allowed, scores, NEGATIVE)
        before = m_ref[rows]
        newest = jnp.maximum(before, jnp.max(scores, axis=1, keepdims=True))
        factor = jnp.exp2((before - newest) * gain)
        probs = jnp.exp2((scores - newest[:, :1]) * gain)
        if allowed is not None:
            probs = jnp.where(allowed, probs, 0.0)
        m_ref[rows] = newest
        l_ref[rows] = l_ref[rows] * factor + jnp.sum(probs, axis=1, keepdims=True)
        acc_ref[rows] = acc_ref[rows] * factor + jnp.dot(
            probs.astype(BF), values, preferred_element_type=F32
        )

    def cached(ref, base):
        def one(number, unused):
            first = base + number * KEYS
            rows = pl.ds(pl.multiple_of(number * KEYS, KEYS), KEYS)
            place = first + lax.broadcasted_iota(jnp.int32, (SUB, KEYS), 1)
            for sub in range(subs):
                absorb(sub, ref[rows, :hd], ref[rows, hd:], place < length)
            return unused

        lax.fori_loop(0, ref.shape[0] // KEYS, one, 0)

    reach = co_ref.shape[0]
    cached(co_ref, rep * reach)
    cached(cx_ref, (1 - rep) * reach)
    tok = meta_tok(q_ref.shape[0])
    row = lax.broadcasted_iota(jnp.int32, (SUB, SUB), 0)
    column = lax.broadcasted_iota(jnp.int32, (SUB, SUB), 1)
    own_ok = column <= row
    other_ok = column // tok < row // tok + rep
    for number in range(subs):
        rows = pl.ds(number * SUB, SUB)
        for ref, allowed in ((fo_ref, own_ok), (fx_ref, other_ok)):
            for sub in range(number, subs):
                absorb(
                    sub, ref[rows, :hd], ref[rows, hd:], allowed if sub == number else None
                )
    o_ref[...] = (acc_ref[...] / l_ref[...]).astype(o_ref.dtype)
    for _ in copies:
        pass


def meta_tok(rows):
    return rows // (NX * NZ)


def attend(meta, queries, cache_own, cache_other, fresh_own, fresh_other, number):
    rows, hd = queries.shape
    count = NX * NZ
    per = count // 2
    (crows, width), frows = cache_own.shape, fresh_own.shape[0]
    return pl.pallas_call(
        attend_kernel,
        out_shape=(
            jax.ShapeDtypeStruct((rows, hd), BF),
            jax.ShapeDtypeStruct((2, per, crows // count, width), BF),
            jax.ShapeDtypeStruct((2, per, frows // count, width), BF),
        ),
        in_specs=[pl.BlockSpec(memory_space=pltpu.SMEM)] + [VMEM_ALL] * 5,
        out_specs=(VMEM_ALL, ANY, ANY),
        scratch_shapes=[pltpu.VMEM((rows, hd), F32)] * 3
        + [
            pltpu.SemaphoreType.DMA((2, count)),
            pltpu.SemaphoreType.DMA((2, 2, per)),
        ],
        compiler_params=pltpu.CompilerParams(
            collective_id=number, has_side_effects=True, vmem_limit_bytes=16 << 20
        ),
        cost_estimate=pl.CostEstimate(
            flops=4 * rows * hd * 5120,
            bytes_accessed=4 << 20,
            transcendentals=rows * 5120,
        ),
        name="attend",
    )(meta, queries, cache_own, cache_other, fresh_own, fresh_other)


def gather_rows(weight, rep_index):
    half = weight.shape[0] // 2
    mine = lax.dynamic_slice_in_dim(weight, rep_index * half, half, 0)
    return lax.all_gather(mine, ROW + ("core",), axis=0, tiled=True)


def swap(value):
    return lax.ppermute(value, "core", [(0, 1), (1, 0)])


def on_device(streams, lengths, cache, hc_static, hc_dynamic, w_qkv, w_out, w_gate_up, w_down):
    rep_count = 2
    col_count = NX * NZ
    rep_index = lax.axis_index("core")
    tok_dev, stream_count, width = streams.shape
    tok_rep = tok_dev * col_count
    head_dim = w_qkv.shape[2] // 3
    length = lengths[0]
    cache = cache[0, 0]
    cache_other = swap(cache)
    head_rows = gather_rows(jnp.concatenate([w_qkv[:, 0, :], w_out], axis=1), rep_index)
    qkv_rows, out_rows = head_rows[:, : 3 * head_dim], head_rows[:, 3 * head_dim :]
    streams = with_layout_constraint(
        jnp.transpose(streams, (1, 0, 2)), Layout(major_to_minor=(0, 1, 2))
    )
    streams = lax.optimization_barrier(streams)
    mix_attn, normed_attn = connect(streams, hc_static[0], hc_dynamic[0])
    input_attn = gather_tokens(normed_attn, 0).reshape(tok_rep, width)
    projected = jnp.dot(input_attn, qkv_rows, preferred_element_type=F32)
    row_ids = jnp.arange(tok_rep, dtype=jnp.int32)
    stretch_ids = (row_ids // tok_dev * rep_count + rep_index) * tok_dev + row_ids % tok_dev
    cosine, sine = rope_tables(length + stretch_ids, head_dim)
    queries = rotate(projected[:, :head_dim], cosine, sine).astype(BF)
    key_new = rotate(projected[:, head_dim : 2 * head_dim], cosine, sine).astype(BF)
    value_new = projected[:, 2 * head_dim :].astype(BF)
    fresh = jnp.concatenate([key_new, value_new], axis=1)
    fresh_other = swap(fresh)
    attended, decode_cache, decode_new = attend(
        lengths, queries, cache, cache_other, fresh, fresh_other, 4
    )
    attn_partial = lax.dot_general(
        attended, out_rows, (((1,), (1,)), ((), ())), preferred_element_type=F32
    ).astype(BF)
    attn_branch = scatter_sum(attn_partial.reshape(col_count, tok_dev, width), 1)
    streams_mid = blend(mix_attn, streams, attn_branch)
    mix_ffn, normed_ffn = connect(streams_mid, hc_static[1], hc_dynamic[1])
    input_ffn = gather_tokens(normed_ffn, 2).reshape(tok_rep, width)
    gate_rows = gather_rows(w_gate_up, rep_index)
    down_rows = gather_rows(w_down, rep_index)
    gate_up = jnp.einsum("td,dkf->tkf", input_ffn, gate_rows, preferred_element_type=F32)
    hidden = (jax.nn.silu(gate_up[:, 0]) * gate_up[:, 1]).astype(BF)
    ffn_partial = lax.dot_general(
        hidden, down_rows, (((1,), (1,)), ((), ())), preferred_element_type=F32
    ).astype(BF)
    ffn_branch = scatter_sum(ffn_partial.reshape(col_count, tok_dev, width), 3)
    new_streams = jnp.transpose(blend(mix_ffn, streams_mid, ffn_branch), (1, 0, 2))
    return (new_streams, decode_cache[None], decode_new[None])


def solution(mesh):
    rows = mesh.devices.shape[0]
    fine = Mesh(
        mesh.devices.reshape((2, rows // 2, NX, NZ, 2)), ("zl", "y", "x", "zh", "core")
    )
    placed = (
        P(ROW + COL + ("core",), None, None),
        P(ROW),
        P(ROW, COL, "core", None),
        P(),
        P(),
        P(ROW, COL, None),
        P(ROW, COL),
        P(ROW, None, COL),
        P(ROW, COL),
    )
    return jax.shard_map(
        on_device,
        mesh=fine,
        in_specs=placed,
        out_specs=(
            P(ROW + COL + ("core",), None, None),
            P(ROW, None, "core", COL, None),
            P(ROW, None, "core", COL, None),
        ),
        check_vma=False,
    )
```

```python
import functools
import math

import jax
import jax.numpy as jnp
from jax import lax
from jax.experimental import pallas as pl
from jax.experimental.layout import Layout, with_layout_constraint
from jax.experimental.pallas import tpu as pltpu
from jax.sharding import Mesh
from jax.sharding import PartitionSpec as P

EPS = 1e-05
NEGATIVE = -1e30
MESH = pl.DeviceIdType.MESH
ROW = ("zl", "y")
COL = ("x", "zh")
NX = 4
NZ = 4
BF = jnp.bfloat16
F32 = jnp.float32
VMEM_ALL = pl.BlockSpec(memory_space=pltpu.VMEM)
ANY = pl.BlockSpec(memory_space=pl.ANY)


def rope_tables(positions, rot_width):
    half_width = rot_width // 2
    inverse = jnp.exp(
        -jnp.log(10000.0) * (2.0 * jnp.arange(half_width, dtype=F32) / rot_width)
    )
    angles = positions.astype(F32)[:, None] * inverse[None, :]
    return jnp.cos(angles), jnp.sin(angles)


def rotate(values, cosine, sine):
    half_width = values.shape[-1] // 2
    first, second = values[:, :half_width], values[:, half_width:]
    return jnp.concatenate(
        [first * cosine - second * sine, second * cosine + first * sine], axis=-1
    )


def connect(streams, static, dynamic):
    widened = streams.astype(F32)
    products = jnp.einsum("std,dk->stk", streams, dynamic, preferred_element_type=F32)
    stream_rms = jnp.sqrt(jnp.mean(widened * widened, axis=2) + EPS)
    weights = static[:, None] + jnp.tanh(products / stream_rms[:, :, None])
    mixture = jnp.sum(weights[:, :, 0:1] * widened, axis=0)
    center = jnp.mean(mixture, axis=1, keepdims=True)
    spread = jnp.mean(mixture * mixture, axis=1, keepdims=True) - center * center
    normed = ((mixture - center) / jnp.sqrt(spread + EPS)).astype(BF)
    return (weights, normed)


def blend(weights, streams, branch):
    stream_count = streams.shape[0]
    widened = streams.astype(F32)
    outputs = []
    for target in range(stream_count):
        carried = jnp.sum(weights[:, :, 1 + target][:, :, None] * widened, axis=0)
        outputs.append(carried + weights[target, :, stream_count + 1][:, None] * branch)
    return jnp.stack(outputs, axis=0).astype(BF)


def around():
    x, z = lax.axis_index("x"), lax.axis_index("zh")
    return (
        x,
        z,
        lax.rem(x + 1, NX),
        lax.rem(x + NX - 1, NX),
        lax.rem(z + 1, NZ),
        lax.rem(z + NZ - 1, NZ),
    )


def greet(places):
    barrier = pltpu.get_barrier_semaphore()
    for place in places:
        pl.semaphore_signal(barrier, inc=1, device_id=place, device_id_type=MESH)
    pl.semaphore_wait(barrier, len(places))


def places():
    x, z, xr, xl, zu, zd = around()
    x2, z2 = lax.rem(x + 2, NX), lax.rem(z + 2, NZ)
    return {"x": (x, xr, xl, x2), "zh": (z, zu, zd, z2)}


def slot_of(first, i, j):
    return i * NZ + j if first == "x" else j * NZ + i


def neighbours(position):
    return [{axis: position[axis][step]} for axis in ("x", "zh") for step in (1, 2)]


def cut(width):
    return (0, width - width * 3 // 16), (width - width * 3 // 16, width * 3 // 16)


def take_turns(left, right):
    for _ in left:
        next(right, None)
    for _ in right:
        pass


def gather_kernel(t_ref, o_ref, send_sem, recv_sem, own_sem):
    position = places()
    half = t_ref.shape[0] // 2
    top, low = pl.ds(0, half), pl.ds(half, half)
    whole = pl.ds(0, 2 * half)
    mine = position["x"][0] * NZ + position["zh"][0]
    greet(neighbours(position))
    started = []

    def part(base, first, second, columns):
        p, pn, pp, p2 = position[first]
        q, qn, qp, q2 = position[second]
        right, left, up, down = {second: qn}, {second: qp}, {first: pn}, {first: pp}
        cols = pl.ds(*columns)

        def at(i, j):
            return slot_of(first, i, j)

        def copy(kind, own, slot, rows, place):
            src = t_ref.at[rows, cols] if own else o_ref.at[slot, rows, cols]
            return pltpu.make_async_remote_copy(
                src_ref=src,
                dst_ref=o_ref.at[slot, rows, cols],
                send_sem=send_sem.at[base + kind],
                recv_sem=recv_sem.at[base + kind],
                device_id=place,
                device_id_type=MESH,
            )

        def start(*given):
            made = copy(*given)
            made.start()
            started.append(made)

        def arrived(kind, rows, place):
            copy(kind, True, mine, rows, place).wait_recv()

        start(0, True, mine, whole, up)
        start(1, True, mine, whole, down)
        yield
        start(4, True, mine, whole, right)
        start(5, True, mine, whole, left)
        yield
        below, above, far = at(pp, q), at(pn, q), at(p2, q)
        arrived(0, whole, up)
        start(2, False, below, top, up)
        start(8, False, below, whole, right)
        start(9, False, below, whole, left)
        arrived(1, whole, down)
        start(3, False, above, low, down)
        start(12, False, above, whole, right)
        start(13, False, above, whole, left)
        yield
        ring = (p, pp, pn, p2)

        def relay(j):
            arrived(4 + 4 * j, whole, right)
            start(6 + 4 * j, False, at(ring[j], qp), top, right)
            arrived(5 + 4 * j, whole, left)
            start(7 + 4 * j, False, at(ring[j], qn), low, left)

        relay(0)
        yield
        arrived(2, top, up)
        arrived(3, low, down)
        start(16, False, far, whole, right)
        start(17, False, far, whole, left)
        yield
        for j in range(1, 4):
            relay(j)
            yield
        for j in range(4):
            arrived(6 + 4 * j, top, right)
            arrived(7 + 4 * j, low, left)

    most, rest = cut(t_ref.shape[1])
    along_z = part(0, "zh", "x", most)
    along_x = part(20, "x", "zh", rest)
    next(along_x)
    next(along_z)
    own = pltpu.make_async_copy(t_ref, o_ref.at[mine], own_sem)
    own.start()
    take_turns(along_z, along_x)
    own.wait()
    for made in started:
        made.wait_send()


def gather_tokens(block, number):
    rows, width = block.shape
    return pl.pallas_call(
        gather_kernel,
        out_shape=jax.ShapeDtypeStruct((NX * NZ, rows, width), BF),
        in_specs=[VMEM_ALL],
        out_specs=VMEM_ALL,
        scratch_shapes=[
            pltpu.SemaphoreType.DMA((40,)),
            pltpu.SemaphoreType.DMA((40,)),
            pltpu.SemaphoreType.DMA,
        ],
        compiler_params=pltpu.CompilerParams(
            collective_id=number, has_side_effects=True, vmem_limit_bytes=48 << 20
        ),
        name="gather_tokens",
    )(block)


def scatter_kernel(p_ref, o_ref, *scratch):
    send_sem, recv_sem = scratch[-2:]
    position = places()
    half = p_ref.shape[1] // 2
    top, low = pl.ds(0, half), pl.ds(half, half)
    greet(neighbours(position))
    started = []

    def wide(ref):
        return ref[...].astype(F32)

    def part(base, first, second, columns, xin, xsum, tin, total, tsum):
        p, pn, pp, p2 = position[first]
        q, qn, qp, q2 = position[second]
        right, left, up, down = {first: pn}, {first: pp}, {second: qn}, {second: qp}
        cols = pl.ds(*columns)
        ring = (q2, qn, qp, q)

        def term(i, j, rows):
            return p_ref.at[slot_of(first, i, ring[j]), rows, cols]

        def copy(kind, src, dst, place):
            return pltpu.make_async_remote_copy(
                src_ref=src,
                dst_ref=dst,
                send_sem=send_sem.at[base + kind],
                recv_sem=recv_sem.at[base + kind],
                device_id=place,
                device_id_type=MESH,
            )

        def start(*given):
            made = copy(*given)
            made.start()
            started.append(made)

        def arrived(kind, ref, place):
            copy(kind, ref, ref, place).wait_recv()

        def distant(j):
            start(6 * j, term(p2, j, top), xin.at[j, 0], right)
            start(6 * j + 1, term(p2, j, low), xin.at[j, 1], left)

        def near(j):
            start(6 * j + 2, term(pn, j, low), xin.at[j, 2], right)
            start(6 * j + 3, term(pp, j, top), xin.at[j, 3], left)

        def pass_on(j):
            arrived(6 * j, xin.at[j, 0], right)
            xsum[j, 0] = (wide(term(pn, j, top)) + wide(xin.at[j, 0])).astype(BF)
            start(6 * j + 4, xsum.at[j, 0], xin.at[j, 4], right)
            arrived(6 * j + 1, xin.at[j, 1], left)
            xsum[j, 1] = (wide(term(pp, j, low)) + wide(xin.at[j, 1])).astype(BF)
            start(6 * j + 5, xsum.at[j, 1], xin.at[j, 5], left)
            if j < 2:
                distant(j + 2)
            if j < 3:
                near(j + 1)

        def finish(j):
            for kind, place in ((2, right), (3, left), (4, right), (5, left)):
                arrived(6 * j + kind, xin.at[j, kind], place)
            a = wide(term(p, j, top)) + wide(xin.at[j, 4]) + wide(xin.at[j, 3])
            b = wide(term(p, j, low)) + wide(xin.at[j, 2]) + wide(xin.at[j, 5])
            return a, b

        last = 24
        distant(0)
        distant(1)
        near(0)
        yield
        pass_on(0)
        yield
        pass_on(1)
        yield
        a, b = finish(0)
        total[0, 0], total[0, 1] = a.astype(BF), b.astype(BF)
        start(last, total.at[0, 0], tin.at[0], up)
        start(last + 1, total.at[0, 1], tin.at[1], down)
        yield
        pass_on(2)
        yield
        a, b = finish(1)
        total[1, 1] = b.astype(BF)
        start(last + 2, total.at[1, 1], tin.at[2], up)
        arrived(last, tin.at[0], up)
        tsum[0] = (a + wide(tin.at[0])).astype(BF)
        start(last + 4, tsum.at[0], tin.at[4], up)
        yield
        pass_on(3)
        yield
        a, b = finish(2)
        total[2, 0] = a.astype(BF)
        start(last + 3, total.at[2, 0], tin.at[3], down)
        arrived(last + 1, tin.at[1], down)
        tsum[1] = (b + wide(tin.at[1])).astype(BF)
        start(last + 5, tsum.at[1], tin.at[5], down)
        yield
        a, b = finish(3)
        for kind, place in ((2, up), (3, down), (4, up), (5, down)):
            arrived(last + kind, tin.at[kind], place)
        o_ref[top, cols] = a + wide(tin.at[4]) + wide(tin.at[3])
        o_ref[low, cols] = b + wide(tin.at[2]) + wide(tin.at[5])

    most, rest = cut(p_ref.shape[2])
    take_turns(
        part(0, "x", "zh", most, *scratch[:5]), part(30, "zh", "x", rest, *scratch[5:10])
    )
    for made in started:
        made.wait_send()


def scatter_sum(partial, number):
    blocks, rows, width = partial.shape
    half = rows // 2
    buffers = []
    for first, size in cut(width):
        for lead in ((4, 6), (4, 2), (6,), (3, 2), (2,)):
            buffers.append(pltpu.VMEM(lead + (half, size), BF))
    return pl.pallas_call(
        scatter_kernel,
        out_shape=jax.ShapeDtypeStruct((rows, width), F32),
        in_specs=[VMEM_ALL],
        out_specs=VMEM_ALL,
        scratch_shapes=buffers
        + [pltpu.SemaphoreType.DMA((60,)), pltpu.SemaphoreType.DMA((60,))],
        compiler_params=pltpu.CompilerParams(
            collective_id=number, has_side_effects=True, vmem_limit_bytes=48 << 20
        ),
        name="scatter_sum",
    )(partial)


def decode_copies(c_ref, f_ref, dc_ref, dn_ref, send_sem, recv_sem):
    x, z, e = lax.axis_index("x"), lax.axis_index("zh"), lax.axis_index("core")
    col = x * NZ + z
    count = NX * NZ
    per = dc_ref.shape[1]
    crows, frows = dc_ref.shape[2], dn_ref.shape[2]
    to_core, slot = col // per, lax.rem(col, per)
    barrier = pltpu.get_barrier_semaphore()

    def at(c, core):
        return {"x": c // NZ, "zh": lax.rem(c, NZ), "core": core}

    for s in range(per):
        source = e * per + lax.rem(slot + s, per)
        for core in range(2):

            @pl.when(jnp.logical_not(jnp.logical_and(source == col, e == core)))
            def _():
                pl.semaphore_signal(
                    barrier, inc=1, device_id=at(source, core), device_id_type=MESH
                )

    stays = (to_core == e).astype(jnp.int32)
    pl.semaphore_wait(barrier, count - stays)

    def pieces(c):
        return (
            (c_ref.at[pl.ds(pl.multiple_of(c * crows, crows), crows)], dc_ref.at[e, slot]),
            (f_ref.at[pl.ds(pl.multiple_of(c * frows, frows), frows)], dn_ref.at[e, slot]),
        )

    def remote(s, kind):
        c = lax.rem(col + s, count)
        src, dst = pieces(c)[kind]
        return pltpu.make_async_remote_copy(
            src_ref=src,
            dst_ref=dst,
            send_sem=send_sem.at[kind, s],
            recv_sem=recv_sem.at[kind, e, slot],
            device_id=at(c, to_core),
            device_id_type=MESH,
        )

    def local(kind):
        src, dst = pieces(col)[kind]
        return pltpu.make_async_copy(src, dst, send_sem.at[kind, 0])

    for s in range(1, count):
        for kind in range(2):
            remote(s, kind).start()
    for kind in range(2):

        @pl.when(to_core == e)
        def _():
            local(kind).start()

        @pl.when(to_core != e)
        def _():
            remote(0, kind).start()

    yield
    for core in range(2):
        for i in range(per):
            for kind, ref in ((0, dc_ref), (1, dn_ref)):

                @pl.when(jnp.logical_not(jnp.logical_and(core == e, e * per + i == col)))
                def _():
                    pltpu.make_async_remote_copy(
                        src_ref=ref.at[core, i],
                        dst_ref=ref.at[core, i],
                        send_sem=send_sem.at[kind, 0],
                        recv_sem=recv_sem.at[kind, core, i],
                        device_id=at(col, 1 - e),
                        device_id_type=MESH,
                    ).wait_recv()

    for s in range(1, count):
        for kind in range(2):
            remote(s, kind).wait_send()
    for kind in range(2):

        @pl.when(to_core == e)
        def _():
            local(kind).wait()

        @pl.when(to_core != e)
        def _():
            remote(0, kind).wait_send()


SUB = 256
KEYS = 512


def attend_kernel(
    meta, q_ref, co_ref, cx_ref, fo_ref, fx_ref, o_ref, dc_ref, dn_ref,
    m_ref, l_ref, acc_ref, send_sem, recv_sem,
):
    hd = q_ref.shape[1]
    subs = q_ref.shape[0] // SUB
    gain = 1.0 / (math.sqrt(hd) * math.log(2.0))
    length, rep = meta[0], lax.axis_index("core")
    copies = decode_copies(co_ref, fo_ref, dc_ref, dn_ref, send_sem, recv_sem)
    next(copies)
    m_ref[...] = jnp.full_like(m_ref, NEGATIVE)
    l_ref[...] = jnp.zeros_like(l_ref)
    acc_ref[...] = jnp.zeros_like(acc_ref)

    def absorb(sub, keys, values, allowed):
        rows = pl.ds(sub * SUB, SUB)
        scores = lax.dot_general(
            q_ref[rows], keys, (((1,), (1,)), ((), ())), preferred_element_type=F32
        )
        if allowed is not None:
            scores = jnp.where(allowed, scores, NEGATIVE)
        before = m_ref[rows]
        newest = jnp.maximum(before, jnp.max(scores, axis=1, keepdims=True))
        factor = jnp.exp2((before - newest) * gain)
        probs = jnp.exp2((scores - newest[:, :1]) * gain)
        if allowed is not None:
            probs = jnp.where(allowed, probs, 0.0)
        m_ref[rows] = newest
        l_ref[rows] = l_ref[rows] * factor + jnp.sum(probs, axis=1, keepdims=True)
        acc_ref[rows] = acc_ref[rows] * factor + jnp.dot(
            probs.astype(BF), values, preferred_element_type=F32
        )

    def cached(ref, base):
        def one(number, unused):
            first = base + number * KEYS
            rows = pl.ds(pl.multiple_of(number * KEYS, KEYS), KEYS)
            place = first + lax.broadcasted_iota(jnp.int32, (SUB, KEYS), 1)
            for sub in range(subs):
                absorb(sub, ref[rows, :hd], ref[rows, hd:], place < length)
            return unused

        lax.fori_loop(0, ref.shape[0] // KEYS, one, 0)

    reach = co_ref.shape[0]
    cached(co_ref, rep * reach)
    cached(cx_ref, (1 - rep) * reach)
    tok = meta_tok(q_ref.shape[0])
    row = lax.broadcasted_iota(jnp.int32, (SUB, SUB), 0)
    column = lax.broadcasted_iota(jnp.int32, (SUB, SUB), 1)
    own_ok = column <= row
    other_ok = column // tok < row // tok + rep
    for number in range(subs):
        rows = pl.ds(number * SUB, SUB)
        for ref, allowed in ((fo_ref, own_ok), (fx_ref, other_ok)):
            for sub in range(number, subs):
                absorb(
                    sub, ref[rows, :hd], ref[rows, hd:], allowed if sub == number else None
                )
    o_ref[...] = (acc_ref[...] / l_ref[...]).astype(o_ref.dtype)
    for _ in copies:
        pass


def meta_tok(rows):
    return rows // (NX * NZ)


def attend(meta, queries, cache_own, cache_other, fresh_own, fresh_other, number):
    rows, hd = queries.shape
    count = NX * NZ
    per = count // 2
    (crows, width), frows = cache_own.shape, fresh_own.shape[0]
    return pl.pallas_call(
        attend_kernel,
        out_shape=(
            jax.ShapeDtypeStruct((rows, hd), BF),
            jax.ShapeDtypeStruct((2, per, crows // count, width), BF),
            jax.ShapeDtypeStruct((2, per, frows // count, width), BF),
        ),
        in_specs=[pl.BlockSpec(memory_space=pltpu.SMEM)] + [VMEM_ALL] * 5,
        out_specs=(VMEM_ALL, ANY, ANY),
        scratch_shapes=[pltpu.VMEM((rows, hd), F32)] * 3
        + [
            pltpu.SemaphoreType.DMA((2, count)),
            pltpu.SemaphoreType.DMA((2, 2, per)),
        ],
        compiler_params=pltpu.CompilerParams(
            collective_id=number, has_side_effects=True, vmem_limit_bytes=16 << 20
        ),
        cost_estimate=pl.CostEstimate(
            flops=4 * rows * hd * 5120,
            bytes_accessed=4 << 20,
            transcendentals=rows * 5120,
        ),
        name="attend",
    )(meta, queries, cache_own, cache_other, fresh_own, fresh_other)


def gather_rows(weight, rep_index):
    half = weight.shape[0] // 2
    mine = lax.dynamic_slice_in_dim(weight, rep_index * half, half, 0)
    return lax.all_gather(mine, ROW + ("core",), axis=0, tiled=True)


def swap(value):
    return lax.ppermute(value, "core", [(0, 1), (1, 0)])


def on_device(streams, lengths, cache, hc_static, hc_dynamic, w_qkv, w_out, w_gate_up, w_down):
    rep_count = 2
    col_count = NX * NZ
    rep_index = lax.axis_index("core")
    tok_dev, stream_count, width = streams.shape
    tok_rep = tok_dev * col_count
    head_dim = w_qkv.shape[2] // 3
    length = lengths[0]
    cache = cache[0, 0]
    cache_other = swap(cache)
    head_rows = gather_rows(jnp.concatenate([w_qkv[:, 0, :], w_out], axis=1), rep_index)
    qkv_rows, out_rows = head_rows[:, : 3 * head_dim], head_rows[:, 3 * head_dim :]
    streams = with_layout_constraint(
        jnp.transpose(streams, (1, 0, 2)), Layout(major_to_minor=(0, 1, 2))
    )
    streams = lax.optimization_barrier(streams)
    mix_attn, normed_attn = connect(streams, hc_static[0], hc_dynamic[0])
    input_attn = gather_tokens(normed_attn, 0).reshape(tok_rep, width)
    projected = jnp.dot(input_attn, qkv_rows, preferred_element_type=F32)
    row_ids = jnp.arange(tok_rep, dtype=jnp.int32)
    stretch_ids = (row_ids // tok_dev * rep_count + rep_index) * tok_dev + row_ids % tok_dev
    cosine, sine = rope_tables(length + stretch_ids, head_dim)
    queries = rotate(projected[:, :head_dim], cosine, sine).astype(BF)
    key_new = rotate(projected[:, head_dim : 2 * head_dim], cosine, sine).astype(BF)
    value_new = projected[:, 2 * head_dim :].astype(BF)
    fresh = jnp.concatenate([key_new, value_new], axis=1)
    fresh_other = swap(fresh)
    attended, decode_cache, decode_new = attend(
        lengths, queries, cache, cache_other, fresh, fresh_other, 4
    )
    attn_partial = lax.dot_general(
        attended, out_rows, (((1,), (1,)), ((), ())), preferred_element_type=F32
    ).astype(BF)
    attn_branch = scatter_sum(attn_partial.reshape(col_count, tok_dev, width), 1)
    streams_mid = blend(mix_attn, streams, attn_branch)
    mix_ffn, normed_ffn = connect(streams_mid, hc_static[1], hc_dynamic[1])
    input_ffn = gather_tokens(normed_ffn, 2).reshape(tok_rep, width)
    gate_rows = gather_rows(w_gate_up, rep_index)
    down_rows = gather_rows(w_down, rep_index)
    gate_up = jnp.einsum("td,dkf->tkf", input_ffn, gate_rows, preferred_element_type=F32)
    hidden = (jax.nn.silu(gate_up[:, 0]) * gate_up[:, 1]).astype(BF)
    ffn_partial = lax.dot_general(
        hidden, down_rows, (((1,), (1,)), ((), ())), preferred_element_type=F32
    ).astype(BF)
    ffn_branch = scatter_sum(ffn_partial.reshape(col_count, tok_dev, width), 3)
    new_streams = jnp.transpose(blend(mix_ffn, streams_mid, ffn_branch), (1, 0, 2))
    return (new_streams, decode_cache[None], decode_new[None])


def solution(mesh):
    rows = mesh.devices.shape[0]
    fine = Mesh(
        mesh.devices.reshape((2, rows // 2, NX, NZ, 2)), ("zl", "y", "x", "zh", "core")
    )
    placed = (
        P(ROW + COL + ("core",), None, None),
        P(ROW),
        P(ROW, COL, "core", None),
        P(),
        P(),
        P(ROW, COL, None),
        P(ROW, COL),
        P(ROW, None, COL),
        P(ROW, COL),
    )
    return jax.shard_map(
        on_device,
        mesh=fine,
        in_specs=placed,
        out_specs=(
            P(ROW + COL + ("core",), None, None),
            P(ROW, None, "core", COL, None),
            P(ROW, None, "core", COL, None),
        ),
        check_vma=False,
    )
```

```python
import functools
import math

import jax
import jax.numpy as jnp
from jax import lax
from jax.experimental import pallas as pl
from jax.experimental.layout import Layout, with_layout_constraint
from jax.experimental.pallas import tpu as pltpu
from jax.sharding import Mesh
from jax.sharding import PartitionSpec as P

EPS = 1e-05
NEGATIVE = -1e30
MESH = pl.DeviceIdType.MESH
ROW = ("zl", "y")
COL = ("x", "zh")
NX = 4
NZ = 4
BF = jnp.bfloat16
F32 = jnp.float32
VMEM_ALL = pl.BlockSpec(memory_space=pltpu.VMEM)
ANY = pl.BlockSpec(memory_space=pl.ANY)


def rope_tables(positions, rot_width):
    half_width = rot_width // 2
    inverse = jnp.exp(
        -jnp.log(10000.0) * (2.0 * jnp.arange(half_width, dtype=F32) / rot_width)
    )
    angles = positions.astype(F32)[:, None] * inverse[None, :]
    return jnp.cos(angles), jnp.sin(angles)


def rotate(values, cosine, sine):
    half_width = values.shape[-1] // 2
    first, second = values[:, :half_width], values[:, half_width:]
    return jnp.concatenate(
        [first * cosine - second * sine, second * cosine + first * sine], axis=-1
    )


def connect(streams, static, dynamic):
    widened = streams.astype(F32)
    products = jnp.einsum("std,dk->stk", streams, dynamic, preferred_element_type=F32)
    stream_rms = jnp.sqrt(jnp.mean(widened * widened, axis=2) + EPS)
    weights = static[:, None] + jnp.tanh(products / stream_rms[:, :, None])
    mixture = jnp.sum(weights[:, :, 0:1] * widened, axis=0)
    center = jnp.mean(mixture, axis=1, keepdims=True)
    spread = jnp.mean(mixture * mixture, axis=1, keepdims=True) - center * center
    normed = ((mixture - center) / jnp.sqrt(spread + EPS)).astype(BF)
    return (weights, normed)


def blend(weights, streams, branch):
    stream_count = streams.shape[0]
    widened = streams.astype(F32)
    outputs = []
    for target in range(stream_count):
        carried = jnp.sum(weights[:, :, 1 + target][:, :, None] * widened, axis=0)
        outputs.append(carried + weights[target, :, stream_count + 1][:, None] * branch)
    return jnp.stack(outputs, axis=0).astype(BF)


def around():
    x, z = lax.axis_index("x"), lax.axis_index("zh")
    return (
        x,
        z,
        lax.rem(x + 1, NX),
        lax.rem(x + NX - 1, NX),
        lax.rem(z + 1, NZ),
        lax.rem(z + NZ - 1, NZ),
    )


def greet(places):
    barrier = pltpu.get_barrier_semaphore()
    for place in places:
        pl.semaphore_signal(barrier, inc=1, device_id=place, device_id_type=MESH)
    pl.semaphore_wait(barrier, len(places))


def places():
    x, z, xr, xl, zu, zd = around()
    x2, z2 = lax.rem(x + 2, NX), lax.rem(z + 2, NZ)
    return {"x": (x, xr, xl, x2), "zh": (z, zu, zd, z2)}


def slot_of(first, i, j):
    return i * NZ + j if first == "x" else j * NZ + i


def neighbours(position):
    return [{axis: position[axis][step]} for axis in ("x", "zh") for step in (1, 2)]


def cut(width):
    return (0, width - width * 3 // 16), (width - width * 3 // 16, width * 3 // 16)


def take_turns(left, right):
    for _ in left:
        next(right, None)
    for _ in right:
        pass


def gather_kernel(t_ref, o_ref, send_sem, recv_sem, own_sem):
    position = places()
    half = t_ref.shape[0] // 2
    top, low = pl.ds(0, half), pl.ds(half, half)
    whole = pl.ds(0, 2 * half)
    mine = position["x"][0] * NZ + position["zh"][0]
    greet(neighbours(position))
    started = []

    def part(base, first, second, columns):
        p, pn, pp, p2 = position[first]
        q, qn, qp, q2 = position[second]
        right, left, up, down = {second: qn}, {second: qp}, {first: pn}, {first: pp}
        cols = pl.ds(*columns)

        def at(i, j):
            return slot_of(first, i, j)

        def copy(kind, own, slot, rows, place):
            src = t_ref.at[rows, cols] if own else o_ref.at[slot, rows, cols]
            return pltpu.make_async_remote_copy(
                src_ref=src,
                dst_ref=o_ref.at[slot, rows, cols],
                send_sem=send_sem.at[base + kind],
                recv_sem=recv_sem.at[base + kind],
                device_id=place,
                device_id_type=MESH,
            )

        def start(*given):
            made = copy(*given)
            made.start()
            started.append(made)

        def arrived(kind, rows, place):
            copy(kind, True, mine, rows, place).wait_recv()

        start(0, True, mine, whole, up)
        start(1, True, mine, whole, down)
        yield
        start(4, True, mine, whole, right)
        start(5, True, mine, whole, left)
        yield
        below, above, far = at(pp, q), at(pn, q), at(p2, q)
        arrived(0, whole, up)
        start(2, False, below, top, up)
        start(8, False, below, whole, right)
        start(9, False, below, whole, left)
        arrived(1, whole, down)
        start(3, False, above, low, down)
        start(12, False, above, whole, right)
        start(13, False, above, whole, left)
        yield
        ring = (p, pp, pn, p2)

        def relay(j):
            arrived(4 + 4 * j, whole, right)
            start(6 + 4 * j, False, at(ring[j], qp), top, right)
            arrived(5 + 4 * j, whole, left)
            start(7 + 4 * j, False, at(ring[j], qn), low, left)

        relay(0)
        yield
        arrived(2, top, up)
        arrived(3, low, down)
        start(16, False, far, whole, right)
        start(17, False, far, whole, left)
        yield
        for j in range(1, 4):
            relay(j)
            yield
        for j in range(4):
            arrived(6 + 4 * j, top, right)
            arrived(7 + 4 * j, low, left)

    most, rest = cut(t_ref.shape[1])
    along_z = part(0, "zh", "x", most)
    along_x = part(20, "x", "zh", rest)
    next(along_x)
    next(along_z)
    own = pltpu.make_async_copy(t_ref, o_ref.at[mine], own_sem)
    own.start()
    take_turns(along_z, along_x)
    own.wait()
    for made in started:
        made.wait_send()


def gather_tokens(block, number):
    rows, width = block.shape
    return pl.pallas_call(
        gather_kernel,
        out_shape=jax.ShapeDtypeStruct((NX * NZ, rows, width), BF),
        in_specs=[VMEM_ALL],
        out_specs=VMEM_ALL,
        scratch_shapes=[
            pltpu.SemaphoreType.DMA((40,)),
            pltpu.SemaphoreType.DMA((40,)),
            pltpu.SemaphoreType.DMA,
        ],
        compiler_params=pltpu.CompilerParams(
            collective_id=number, has_side_effects=True, vmem_limit_bytes=48 << 20
        ),
        name="gather_tokens",
    )(block)


def scatter_kernel(p_ref, o_ref, *scratch):
    send_sem, recv_sem = scratch[-2:]
    position = places()
    half = p_ref.shape[1] // 2
    top, low = pl.ds(0, half), pl.ds(half, half)
    greet(neighbours(position))
    started = []

    def wide(ref):
        return ref[...].astype(F32)

    def part(base, first, second, columns, xin, xsum, tin, total, tsum):
        p, pn, pp, p2 = position[first]
        q, qn, qp, q2 = position[second]
        right, left, up, down = {first: pn}, {first: pp}, {second: qn}, {second: qp}
        cols = pl.ds(*columns)
        ring = (q2, qn, qp, q)

        def term(i, j, rows):
            return p_ref.at[slot_of(first, i, ring[j]), rows, cols]

        def copy(kind, src, dst, place):
            return pltpu.make_async_remote_copy(
                src_ref=src,
                dst_ref=dst,
                send_sem=send_sem.at[base + kind],
                recv_sem=recv_sem.at[base + kind],
                device_id=place,
                device_id_type=MESH,
            )

        def start(*given):
            made = copy(*given)
            made.start()
            started.append(made)

        def arrived(kind, ref, place):
            copy(kind, ref, ref, place).wait_recv()

        def distant(j):
            start(6 * j, term(p2, j, top), xin.at[j, 0], right)
            start(6 * j + 1, term(p2, j, low), xin.at[j, 1], left)

        def near(j):
            start(6 * j + 2, term(pn, j, low), xin.at[j, 2], right)
            start(6 * j + 3, term(pp, j, top), xin.at[j, 3], left)

        def pass_on(j):
            arrived(6 * j, xin.at[j, 0], right)
            xsum[j, 0] = (wide(term(pn, j, top)) + wide(xin.at[j, 0])).astype(BF)
            start(6 * j + 4, xsum.at[j, 0], xin.at[j, 4], right)
            arrived(6 * j + 1, xin.at[j, 1], left)
            xsum[j, 1] = (wide(term(pp, j, low)) + wide(xin.at[j, 1])).astype(BF)
            start(6 * j + 5, xsum.at[j, 1], xin.at[j, 5], left)
            if j < 2:
                distant(j + 2)
            if j < 3:
                near(j + 1)

        def finish(j):
            for kind, place in ((2, right), (3, left), (4, right), (5, left)):
                arrived(6 * j + kind, xin.at[j, kind], place)
            a = wide(term(p, j, top)) + wide(xin.at[j, 4]) + wide(xin.at[j, 3])
            b = wide(term(p, j, low)) + wide(xin.at[j, 2]) + wide(xin.at[j, 5])
            return a, b

        last = 24
        distant(0)
        distant(1)
        near(0)
        yield
        pass_on(0)
        yield
        pass_on(1)
        yield
        a, b = finish(0)
        total[0, 0], total[0, 1] = a.astype(BF), b.astype(BF)
        start(last, total.at[0, 0], tin.at[0], up)
        start(last + 1, total.at[0, 1], tin.at[1], down)
        yield
        pass_on(2)
        yield
        a, b = finish(1)
        total[1, 1] = b.astype(BF)
        start(last + 2, total.at[1, 1], tin.at[2], up)
        arrived(last, tin.at[0], up)
        tsum[0] = (a + wide(tin.at[0])).astype(BF)
        start(last + 4, tsum.at[0], tin.at[4], up)
        yield
        pass_on(3)
        yield
        a, b = finish(2)
        total[2, 0] = a.astype(BF)
        start(last + 3, total.at[2, 0], tin.at[3], down)
        arrived(last + 1, tin.at[1], down)
        tsum[1] = (b + wide(tin.at[1])).astype(BF)
        start(last + 5, tsum.at[1], tin.at[5], down)
        yield
        a, b = finish(3)
        for kind, place in ((2, up), (3, down), (4, up), (5, down)):
            arrived(last + kind, tin.at[kind], place)
        o_ref[top, cols] = a + wide(tin.at[4]) + wide(tin.at[3])
        o_ref[low, cols] = b + wide(tin.at[2]) + wide(tin.at[5])

    most, rest = cut(p_ref.shape[2])
    take_turns(
        part(0, "x", "zh", most, *scratch[:5]), part(30, "zh", "x", rest, *scratch[5:10])
    )
    for made in started:
        made.wait_send()


def scatter_sum(partial, number):
    blocks, rows, width = partial.shape
    half = rows // 2
    buffers = []
    for first, size in cut(width):
        for lead in ((4, 6), (4, 2), (6,), (3, 2), (2,)):
            buffers.append(pltpu.VMEM(lead + (half, size), BF))
    return pl.pallas_call(
        scatter_kernel,
        out_shape=jax.ShapeDtypeStruct((rows, width), F32),
        in_specs=[VMEM_ALL],
        out_specs=VMEM_ALL,
        scratch_shapes=buffers
        + [pltpu.SemaphoreType.DMA((60,)), pltpu.SemaphoreType.DMA((60,))],
        compiler_params=pltpu.CompilerParams(
            collective_id=number, has_side_effects=True, vmem_limit_bytes=48 << 20
        ),
        name="scatter_sum",
    )(partial)


def decode_copies(
    c_ref, f_ref, dc_ref, dn_ref, c_relay, f_relay, send_sem, recv_sem, pass_sem, relay_sem
):
    x, z, e = lax.axis_index("x"), lax.axis_index("zh"), lax.axis_index("core")
    col = x * NZ + z
    count = NX * NZ
    per = dc_ref.shape[1]
    crows, frows = dc_ref.shape[2], dn_ref.shape[2]
    to_core, slot = col // per, lax.rem(col, per)
    barrier = pltpu.get_barrier_semaphore()
    outs, relays = (dc_ref, dn_ref), (c_relay, f_relay)

    def greet_at(place):
        pl.semaphore_signal(barrier, inc=1, device_id=place, device_id_type=MESH)

    for s in range(1, count):
        c = lax.rem(col + s, count)
        for core in range(2):
            greet_at({"x": c // NZ, "zh": lax.rem(c, NZ), "core": core})
    greet_at({"core": 1 - e})
    pl.semaphore_wait(barrier, 2 * count - 1)

    def piece(kind, c):
        ref, size = ((c_ref, crows), (f_ref, frows))[kind]
        return ref.at[pl.ds(pl.multiple_of(c * size, size), size)]

    def remote(kind, dx, dz):
        tx, tz = lax.rem(x + dx, NX), lax.rem(z + dz, NZ)
        src = piece(kind, tx * NZ + tz)
        if dz == 2:
            via = lax.rem(z + (1 if dx % 2 == 0 else NZ - 1), NZ)
            dst, arrival = relays[kind].at[dx], relay_sem.at[kind, dx]
            place = {"x": tx, "zh": via, "core": e}
        else:
            dst, arrival = outs[kind].at[e, slot], recv_sem.at[kind, e, slot]
            place = {"x": tx, "zh": tz, "core": to_core}
        return pltpu.make_async_remote_copy(
            src_ref=src,
            dst_ref=dst,
            send_sem=send_sem.at[kind, dx * NZ + dz],
            recv_sem=arrival,
            device_id=place,
            device_id_type=MESH,
        )

    def onward(kind, dx):
        step = 1 if dx % 2 == 0 else NZ - 1
        source = lax.rem(x + NX - dx, NX) * NZ + lax.rem(z + NZ - step, NZ)
        there = lax.rem(source, per)
        return pltpu.make_async_remote_copy(
            src_ref=relays[kind].at[dx],
            dst_ref=outs[kind].at[e, there],
            send_sem=pass_sem.at[kind, dx],
            recv_sem=recv_sem.at[kind, e, there],
            device_id={"x": x, "zh": lax.rem(z + step, NZ), "core": source // per},
            device_id_type=MESH,
        )

    def local(kind):
        return pltpu.make_async_copy(
            piece(kind, col), outs[kind].at[e, slot], send_sem.at[kind, 0]
        )

    order = [(dx, dz) for dz in (2, 1, 3, 0) for dx in range(NX) if (dx, dz) != (0, 0)]
    for dx, dz in order:
        for kind in range(2):
            remote(kind, dx, dz).start()
    for kind in range(2):

        @pl.when(to_core == e)
        def _():
            local(kind).start()

        @pl.when(to_core != e)
        def _():
            remote(kind, 0, 0).start()

    yield
    for dx in range(NX):
        for kind in range(2):
            remote(kind, dx, 2).wait_recv()
            onward(kind, dx).start()
    yield
    for core in range(2):
        for i in range(per):
            for kind, ref in enumerate(outs):

                @pl.when(jnp.logical_not(jnp.logical_and(core == e, e * per + i == col)))
                def _():
                    pltpu.make_async_remote_copy(
                        src_ref=ref.at[core, i],
                        dst_ref=ref.at[core, i],
                        send_sem=send_sem.at[kind, 0],
                        recv_sem=recv_sem.at[kind, core, i],
                        device_id={"core": 1 - e},
                        device_id_type=MESH,
                    ).wait_recv()

    for kind in range(2):
        for dx, dz in order:
            remote(kind, dx, dz).wait_send()
        for dx in range(NX):
            onward(kind, dx).wait_send()

        @pl.when(to_core == e)
        def _():
            local(kind).wait()

        @pl.when(to_core != e)
        def _():
            remote(kind, 0, 0).wait_send()


SUB = 256
KEYS = 512


def attend_kernel(
    meta, q_ref, c_ref, cx_in, fo_ref, fx_ref, o_ref, dc_ref, dn_ref,
    m_ref, l_ref, acc_ref, co_ref, cx_ref, load_sem, *scratch,
):
    hd = q_ref.shape[1]
    subs = q_ref.shape[0] // SUB
    gain = 1.0 / (math.sqrt(hd) * math.log(2.0))
    length, rep = meta[0], lax.axis_index("core")
    loads = [
        pltpu.make_async_copy(c_ref, co_ref, load_sem.at[0]),
        pltpu.make_async_copy(cx_in, cx_ref, load_sem.at[1]),
    ]
    for load in loads:
        load.start()
    copies = decode_copies(c_ref, fo_ref, dc_ref, dn_ref, *scratch)
    next(copies)
    m_ref[...] = jnp.full_like(m_ref, NEGATIVE)
    l_ref[...] = jnp.zeros_like(l_ref)
    acc_ref[...] = jnp.zeros_like(acc_ref)

    def absorb(sub, keys, values, allowed):
        rows = pl.ds(sub * SUB, SUB)
        scores = lax.dot_general(
            q_ref[rows], keys, (((1,), (1,)), ((), ())), preferred_element_type=F32
        )
        if allowed is not None:
            scores = jnp.where(allowed, scores, NEGATIVE)
        before = m_ref[rows]
        newest = jnp.maximum(before, jnp.max(scores, axis=1, keepdims=True))
        factor = jnp.exp2((before - newest) * gain)
        probs = jnp.exp2((scores - newest[:, :1]) * gain)
        if allowed is not None:
            probs = jnp.where(allowed, probs, 0.0)
        m_ref[rows] = newest
        l_ref[rows] = l_ref[rows] * factor + jnp.sum(probs, axis=1, keepdims=True)
        acc_ref[rows] = acc_ref[rows] * factor + jnp.dot(
            probs.astype(BF), values, preferred_element_type=F32
        )

    def cached(ref, base):
        def one(number, unused):
            first = base + number * KEYS
            rows = pl.ds(pl.multiple_of(number * KEYS, KEYS), KEYS)
            place = first + lax.broadcasted_iota(jnp.int32, (SUB, KEYS), 1)
            for sub in range(subs):
                absorb(sub, ref[rows, :hd], ref[rows, hd:], place < length)
            return unused

        lax.fori_loop(0, ref.shape[0] // KEYS, one, 0)

    tok = meta_tok(q_ref.shape[0])
    row = lax.broadcasted_iota(jnp.int32, (SUB, SUB), 0)
    column = lax.broadcasted_iota(jnp.int32, (SUB, SUB), 1)
    own_ok = column <= row
    other_ok = column // tok < row // tok + rep
    for number in range(subs):
        rows = pl.ds(number * SUB, SUB)
        for ref, allowed in ((fo_ref, own_ok), (fx_ref, other_ok)):
            for sub in range(number, subs):
                absorb(
                    sub, ref[rows, :hd], ref[rows, hd:], allowed if sub == number else None
                )
    reach = co_ref.shape[0]
    loads[0].wait()
    cached(co_ref, rep * reach)
    next(copies)
    loads[1].wait()
    cached(cx_ref, (1 - rep) * reach)
    o_ref[...] = (acc_ref[...] / l_ref[...]).astype(o_ref.dtype)
    for _ in copies:
        pass


def meta_tok(rows):
    return rows // (NX * NZ)


def attend(meta, queries, cache_own, cache_other, fresh_own, fresh_other, number):
    rows, hd = queries.shape
    count = NX * NZ
    per = count // 2
    (crows, width), frows = cache_own.shape, fresh_own.shape[0]
    return pl.pallas_call(
        attend_kernel,
        out_shape=(
            jax.ShapeDtypeStruct((rows, hd), BF),
            jax.ShapeDtypeStruct((2, per, crows // count, width), BF),
            jax.ShapeDtypeStruct((2, per, frows // count, width), BF),
        ),
        in_specs=[pl.BlockSpec(memory_space=pltpu.SMEM), VMEM_ALL, ANY, ANY, VMEM_ALL, VMEM_ALL],
        out_specs=(VMEM_ALL, ANY, ANY),
        scratch_shapes=[pltpu.VMEM((rows, hd), F32)] * 3
        + [pltpu.VMEM((crows, width), BF)] * 2
        + [
            pltpu.SemaphoreType.DMA((2,)),
            pltpu.VMEM((NX, crows // count, width), BF),
            pltpu.VMEM((NX, frows // count, width), BF),
            pltpu.SemaphoreType.DMA((2, count)),
            pltpu.SemaphoreType.DMA((2, 2, per)),
            pltpu.SemaphoreType.DMA((2, NX)),
            pltpu.SemaphoreType.DMA((2, NX)),
        ],
        compiler_params=pltpu.CompilerParams(
            collective_id=number, has_side_effects=True, vmem_limit_bytes=16 << 20
        ),
        cost_estimate=pl.CostEstimate(
            flops=4 * rows * hd * 5120,
            bytes_accessed=4 << 20,
            transcendentals=rows * 5120,
        ),
        name="attend",
    )(meta, queries, cache_own, cache_other, fresh_own, fresh_other)


def gather_rows(weight, rep_index):
    half = weight.shape[0] // 2
    mine = lax.dynamic_slice_in_dim(weight, rep_index * half, half, 0)
    return lax.all_gather(mine, ROW + ("core",), axis=0, tiled=True)


def swap(value):
    return lax.ppermute(value, "core", [(0, 1), (1, 0)])


def on_device(streams, lengths, cache, hc_static, hc_dynamic, w_qkv, w_out, w_gate_up, w_down):
    rep_count = 2
    col_count = NX * NZ
    rep_index = lax.axis_index("core")
    tok_dev, stream_count, width = streams.shape
    tok_rep = tok_dev * col_count
    head_dim = w_qkv.shape[2] // 3
    length = lengths[0]
    cache = cache[0, 0]
    cache_other = swap(cache)
    head_rows = gather_rows(jnp.concatenate([w_qkv[:, 0, :], w_out], axis=1), rep_index)
    qkv_rows, out_rows = head_rows[:, : 3 * head_dim], head_rows[:, 3 * head_dim :]
    streams = with_layout_constraint(
        jnp.transpose(streams, (1, 0, 2)), Layout(major_to_minor=(0, 1, 2))
    )
    streams = lax.optimization_barrier(streams)
    mix_attn, normed_attn = connect(streams, hc_static[0], hc_dynamic[0])
    input_attn = gather_tokens(normed_attn, 0).reshape(tok_rep, width)
    projected = jnp.dot(input_attn, qkv_rows, preferred_element_type=F32)
    row_ids = jnp.arange(tok_rep, dtype=jnp.int32)
    stretch_ids = (row_ids // tok_dev * rep_count + rep_index) * tok_dev + row_ids % tok_dev
    cosine, sine = rope_tables(length + stretch_ids, head_dim)
    queries = rotate(projected[:, :head_dim], cosine, sine).astype(BF)
    key_new = rotate(projected[:, head_dim : 2 * head_dim], cosine, sine).astype(BF)
    value_new = projected[:, 2 * head_dim :].astype(BF)
    fresh = jnp.concatenate([key_new, value_new], axis=1)
    fresh_other = swap(fresh)
    attended, decode_cache, decode_new = attend(
        lengths, queries, cache, cache_other, fresh, fresh_other, 4
    )
    attn_partial = lax.dot_general(
        attended, out_rows, (((1,), (1,)), ((), ())), preferred_element_type=F32
    ).astype(BF)
    attn_branch = scatter_sum(attn_partial.reshape(col_count, tok_dev, width), 1)
    streams_mid = blend(mix_attn, streams, attn_branch)
    mix_ffn, normed_ffn = connect(streams_mid, hc_static[1], hc_dynamic[1])
    input_ffn = gather_tokens(normed_ffn, 2).reshape(tok_rep, width)
    gate_rows = gather_rows(w_gate_up, rep_index)
    down_rows = gather_rows(w_down, rep_index)
    gate_up = jnp.einsum("td,dkf->tkf", input_ffn, gate_rows, preferred_element_type=F32)
    hidden = (jax.nn.silu(gate_up[:, 0]) * gate_up[:, 1]).astype(BF)
    ffn_partial = lax.dot_general(
        hidden, down_rows, (((1,), (1,)), ((), ())), preferred_element_type=F32
    ).astype(BF)
    ffn_branch = scatter_sum(ffn_partial.reshape(col_count, tok_dev, width), 3)
    new_streams = jnp.transpose(blend(mix_ffn, streams_mid, ffn_branch), (1, 0, 2))
    return (new_streams, decode_cache[None], decode_new[None])


def solution(mesh):
    rows = mesh.devices.shape[0]
    fine = Mesh(
        mesh.devices.reshape((2, rows // 2, NX, NZ, 2)), ("zl", "y", "x", "zh", "core")
    )
    placed = (
        P(ROW + COL + ("core",), None, None),
        P(ROW),
        P(ROW, COL, "core", None),
        P(),
        P(),
        P(ROW, COL, None),
        P(ROW, COL),
        P(ROW, None, COL),
        P(ROW, COL),
    )
    return jax.shard_map(
        on_device,
        mesh=fine,
        in_specs=placed,
        out_specs=(
            P(ROW + COL + ("core",), None, None),
            P(ROW, None, "core", COL, None),
            P(ROW, None, "core", COL, None),
        ),
        check_vma=False,
    )
```
